256 devices in a mesh: seq: 32 (over z, x_lo, core), chan: 8 (over x_hi, y).
Axes of the slice: x: 4 (x_hi: 2, x_lo: 2; x = x_hi * 2 + x_lo), y: 4, z: 8, core: 2. Of those that a mesh axis runs over, the one named last changes fastest.
Arguments:
- q_gate: float32 [16384, 2048], P('seq', 'chan'), may hold values from -6 to 6
- k_gate: float32 [16384, 2048], P('seq', 'chan'), may hold values from -6 to 6
- values: float32 [16384, 2048], P('seq', 'chan'), may hold values from -6 to 6
- filter_raw: float32 [16384, 128], P('seq'), may hold values from -6 to 6
- grad_out: float32 [16384, 2048], P('seq', 'chan'), may hold values from -6 to 6
Outputs:
- grad_q: float32 [16384, 2048], P('seq', 'chan')
- grad_k: float32 [16384, 2048], P('seq', 'chan')
- grad_v: float32 [16384, 2048], P('seq', 'chan')
- grad_filter: float32 [16384, 128], P('seq')
The draws below stay inside these ranges and needn't reach their ends.
All inputs are finite; a program needn't handle non-finite values.
Results may differ from the reference program's by a relative error of at most 0.0001.
Values sent between devices are 32-bit elements; how exact they have to be, the bound alone decides.
No kernel may reach another device: no remote copies, remote signals or barrier semaphores. Data moves between devices by JAX's collectives and lax.ppermute only.
A program may use at most 64 MiB of HBM per device.

```python
import jax
import jax.numpy as jnp

C = 2048
FILTERS = 128
LENGTH = 16384


def steps_of(own_key, dims, shards, low, top_value):
    level = 1.0
    for dim, shards_of in shards:
        steps = jax.random.uniform(jax.random.fold_in(jax.random.fold_in(own_key, 6), dim), (shards_of,), jnp.float32, low / len(shards), top_value / len(shards))
        level = level * jnp.repeat(jnp.exp(steps), dims[dim] // shards_of).reshape((-1,) + (1,) * (len(dims) - 1 - dim))
    return level


def noise(key, dims, spread, limit, pieces=(), held_as=jnp.bfloat16):
    array = spread * jax.random.normal(key, dims, jnp.float32)
    if pieces:
        array = array * steps_of(key, dims, pieces, -0.22, 0.18)
    return jnp.clip(array, -limit, limit).astype(held_as)


def setup_inputs(seed: int = 0) -> dict:
    key_of = jax.random.split(jax.random.key(seed), 6)
    q_gate = noise(key_of[0], (LENGTH, C), 1.0, 6.0, ((0, 32), (1, 8)), jnp.float32)
    k_gate = noise(key_of[1], (LENGTH, C), 1.0, 6.0, ((0, 32), (1, 8)), jnp.float32)
    values = noise(key_of[2], (LENGTH, C), 1.0, 6.0, ((0, 32), (1, 8)), jnp.float32)
    filter_raw = noise(key_of[3], (LENGTH, FILTERS), 1.0, 6.0, ((0, 32),), jnp.float32)
    grad_out = noise(key_of[4], (LENGTH, C), 1.0, 6.0, ((0, 32), (1, 8)), jnp.float32)
    return dict(q_gate=q_gate, k_gate=k_gate, values=values, filter_raw=filter_raw, grad_out=grad_out)


def reference(q_gate, k_gate, values, filter_raw, grad_out):
    length = q_gate.shape[0]
    total = 2 * length
    scale = length ** -0.5
    filt = jnp.tile(filter_raw, (1, C // FILTERS)) * scale
    gated = k_gate * values
    grad_conv = grad_out * q_gate
    spec_gated = jnp.fft.rfft(gated, n=total, axis=0)
    spec_filt = jnp.fft.rfft(filt, n=total, axis=0)
    spec_grad = jnp.fft.rfft(grad_conv, n=total, axis=0)
    conv = jnp.fft.irfft(spec_filt * spec_gated, n=total, axis=0)[:length]
    grad_gated = jnp.fft.irfft(jnp.conj(spec_filt) * spec_grad, n=total, axis=0)[:length]
    corr = jnp.fft.irfft(jnp.conj(spec_gated) * spec_grad, n=total, axis=0)[:length]
    grad_filter = scale * jnp.sum(corr.reshape(length, C // FILTERS, FILTERS), axis=1)
    grad_q = grad_out * conv
    grad_k = grad_gated * values
    grad_v = grad_gated * k_gate
    return (grad_q.astype(jnp.float32), grad_k.astype(jnp.float32),
            grad_v.astype(jnp.float32), grad_filter.astype(jnp.float32))
```

```python
import functools

import jax
import jax.numpy as jnp
import numpy as np
from jax import lax
from jax.experimental import pallas as pl
from jax.experimental.pallas import tpu as pltpu
from jax.sharding import PartitionSpec as P


SIDE = 128
HALVES = 2
GROUP = 4
QUARTERS = 4
BF = jnp.bfloat16
F32 = jnp.float32


def split_np(table):
    high = table.astype(np.float32).astype(BF)
    low = (table - high.astype(np.float64)).astype(np.float32).astype(BF)
    return high, low


def tables(shards, factor):
    total = SIDE * SIDE
    index = np.arange(SIDE)
    quarter, source = np.divmod(index, shards)
    first = source * QUARTERS + quarter
    coarse = 2.0 * np.pi * np.outer(index + 0.25, first) / SIDE
    high, low = split_np(np.concatenate([np.cos(coarse), -np.sin(coarse)], axis=0))
    into = np.concatenate([high, low, high], axis=1)
    high, low = split_np(np.concatenate([np.cos(coarse.T), -np.sin(coarse.T)], axis=1) * factor)
    back = np.concatenate([high, low, high], axis=1)
    fine = 2.0 * np.pi * (np.outer(index, index) % SIDE) / SIDE
    cos, sin = np.cos(fine), np.sin(fine)
    high, low = split_np(np.block([[cos, -sin], [sin, cos]]))
    ahead = np.concatenate([high, high, low], axis=0)
    high, low = split_np(np.block([[cos, sin], [-sin, cos]]))
    behind = np.concatenate([high, high, low], axis=0)
    turn = 2.0 * np.pi * np.outer(index + 0.25, index) / total
    twist = np.concatenate([np.cos(turn), np.sin(turn)], axis=1).astype(np.float32)
    return into, back, ahead, behind, twist


def halves(value):
    high = value.astype(BF)
    return high, (value - high.astype(F32)).astype(BF)


def dot(left, right):
    return jnp.dot(left, right, preferred_element_type=F32)


def ahead_pair(one, two, into, ahead, twist):
    high, low = halves(jnp.concatenate([one, two], axis=1))
    coarse = dot(into, jnp.concatenate([high, high, low], axis=0))
    cos, sin = twist[:, :SIDE], twist[:, SIDE:]
    rows = []
    for side in range(2):
        real = coarse[:SIDE, side * SIDE : (side + 1) * SIDE]
        imag = coarse[SIDE:, side * SIDE : (side + 1) * SIDE]
        rows.append(
            jnp.concatenate([real * cos + imag * sin, imag * cos - real * sin], axis=1)
        )
    high, low = halves(jnp.concatenate(rows, axis=0))
    return dot(jnp.concatenate([high, low, high], axis=1), ahead)


def behind_pair(spec, back, behind, twist):
    high, low = halves(spec)
    fine = dot(jnp.concatenate([high, low, high], axis=1), behind)
    cos, sin = twist[:, :SIDE], twist[:, SIDE:]
    reals, imags = [], []
    for side in range(2):
        real = fine[side * SIDE : (side + 1) * SIDE, :SIDE]
        imag = fine[side * SIDE : (side + 1) * SIDE, SIDE:]
        reals.append(real * cos - imag * sin)
        imags.append(imag * cos + real * sin)
    turned = jnp.concatenate(
        [jnp.concatenate(reals, axis=1), jnp.concatenate(imags, axis=1)], axis=0
    )
    high, low = halves(turned)
    return dot(back, jnp.concatenate([high, high, low], axis=0))


def product(left, right, conjugate):
    lr, li = left[:, :SIDE], left[:, SIDE:]
    rr, ri = right[:, :SIDE], right[:, SIDE:]
    if conjugate:
        return lr * rr + li * ri, lr * ri - li * rr
    return lr * rr - li * ri, lr * ri + li * rr


def gather_rows(ref, base, step, shards, pitch):
    return jnp.concatenate(
        [ref[pl.ds(base + q * step, shards, stride=pitch), :] for q in range(QUARTERS)], axis=0
    )


def pack_kernel(shards, pitch, k_ref, v_ref, g_ref, q_ref, f_ref, out_ref):
    for q in range(QUARTERS):
        rows = slice(q * SIDE, (q + 1) * SIDE)
        for h in range(HALVES):
            cols = slice(h * SIDE, (h + 1) * SIDE)
            gated = (k_ref[rows, cols] * v_ref[rows, cols]).T
            grad = (g_ref[rows, cols] * q_ref[rows, cols]).T
            for j in range(GROUP):
                own = slice(j * shards, (j + 1) * shards)
                at = q * 8 + h * GROUP + j
                out_ref[pl.ds(at, shards, stride=pitch), :] = gated[own]
                out_ref[pl.ds(32 + at, shards, stride=pitch), :] = grad[own]
        filt = f_ref[rows, :].T
        for j in range(GROUP):
            own = slice(j * shards, (j + 1) * shards)
            out_ref[pl.ds(64 + q * GROUP + j, shards, stride=pitch), :] = filt[own]


def conv_kernel(
    shards, pitch, in_ref, into_ref, back_ref, ahead_ref, behind_ref, twist_ref,
    out_ref, gated_ref, filt_ref,
):
    into, ahead, twist = into_ref[...], ahead_ref[...], twist_ref[...]
    back, behind = back_ref[...], behind_ref[...]
    for pair in range(GROUP // 2):
        slabs = [
            gather_rows(in_ref, 64 + 2 * pair + j, GROUP, shards, pitch) for j in range(2)
        ]
        filt_ref[pl.ds(pair * 2 * SIDE, 2 * SIDE), :] = ahead_pair(*slabs, into, ahead, twist)
    for j in range(GROUP):
        slabs = [gather_rows(in_ref, h * GROUP + j, 8, shards, pitch) for h in range(HALVES)]
        spec = ahead_pair(*slabs, into, ahead, twist)
        gated_ref[pl.ds(j * 2 * SIDE, 2 * SIDE), :] = spec
        filt = filt_ref[pl.ds(j * SIDE, SIDE), :]
        both = [
            jnp.concatenate(product(filt, spec[h * SIDE : (h + 1) * SIDE], False), axis=1)
            for h in range(HALVES)
        ]
        conv = behind_pair(jnp.concatenate(both, axis=0), back, behind, twist)
        for h in range(HALVES):
            for q in range(QUARTERS):
                out_ref[pl.ds(q * 8 + h * GROUP + j, shards, stride=32), :] = conv[
                    q * shards : (q + 1) * shards, h * SIDE : (h + 1) * SIDE
                ]


def corr_kernel(
    shards, pitch, in_ref, gated_ref, into_ref, back_ref, ahead_ref, behind_ref, twist_ref,
    out_ref, grad_ref,
):
    into, ahead, twist = into_ref[...], ahead_ref[...], twist_ref[...]
    back, behind = back_ref[...], behind_ref[...]
    for pair in range(GROUP // 2):
        sums = []
        for j in (2 * pair, 2 * pair + 1):
            slabs = [
                gather_rows(in_ref, 32 + h * GROUP + j, 8, shards, pitch) for h in range(HALVES)
            ]
            spec = ahead_pair(*slabs, into, ahead, twist)
            grad_ref[pl.ds(j * 2 * SIDE, 2 * SIDE), :] = spec
            gated = gated_ref[pl.ds(j * 2 * SIDE, 2 * SIDE), :]
            lower = product(gated[:SIDE], spec[:SIDE], True)
            upper = product(gated[SIDE:], spec[SIDE:], True)
            sums.append(
                jnp.concatenate([lower[0] + upper[0], lower[1] + upper[1]], axis=1)
            )
        corr = behind_pair(jnp.concatenate(sums, axis=0), back, behind, twist)
        for j in range(2):
            for q in range(QUARTERS):
                out_ref[pl.ds((q * 2 + pair) * 2 * shards + j, shards, stride=2), :] = corr[
                    q * shards : (q + 1) * shards, j * SIDE : (j + 1) * SIDE
                ]


def back_kernel(shards, grad_ref, filt_ref, back_ref, behind_ref, twist_ref, out_ref):
    twist, back, behind = twist_ref[...], back_ref[...], behind_ref[...]
    for j in range(GROUP):
        spec = grad_ref[pl.ds(j * 2 * SIDE, 2 * SIDE), :]
        filt = filt_ref[pl.ds(j * SIDE, SIDE), :]
        both = [
            jnp.concatenate(product(filt, spec[h * SIDE : (h + 1) * SIDE], True), axis=1)
            for h in range(HALVES)
        ]
        grad = behind_pair(jnp.concatenate(both, axis=0), back, behind, twist)
        for h in range(HALVES):
            for q in range(QUARTERS):
                out_ref[pl.ds(q * 8 + h * GROUP + j, shards, stride=32), :] = grad[
                    q * shards : (q + 1) * shards, h * SIDE : (h + 1) * SIDE
                ]


def unpack_kernel(shards, in_ref, *refs):
    count = len(refs) // 2
    for q in range(QUARTERS):
        rows = slice(q * SIDE, (q + 1) * SIDE)
        for h in range(HALVES):
            cols = slice(h * SIDE, (h + 1) * SIDE)
            slab = gather_rows(in_ref, q * 8 + h * GROUP, 1, shards, 32).T
            for weight_ref, out_ref in zip(refs[:count], refs[count:]):
                out_ref[rows, cols] = slab * weight_ref[rows, cols]


def filter_kernel(shards, in_ref, out_ref):
    for q in range(QUARTERS):
        slab = jnp.concatenate(
            [
                in_ref[pl.ds((q * 2 + j // 2) * 2 * shards + j % 2, shards, stride=2), :]
                for j in range(GROUP)
            ],
            axis=0,
        )
        out_ref[q * SIDE : (q + 1) * SIDE, :] = slab.T


def call(kernel, outs, args, name, flops=0):
    shapes = [jax.ShapeDtypeStruct(shape, F32) for shape in outs]
    moved = sum(4 * int(np.prod(shape)) for shape in outs) + sum(a.size * a.dtype.itemsize for a in args)
    return pl.pallas_call(
        kernel,
        out_shape=shapes,
        in_specs=[pl.BlockSpec(memory_space=pltpu.VMEM)] * len(args),
        out_specs=[pl.BlockSpec(memory_space=pltpu.VMEM)] * len(outs),
        name=name,
        compiler_params=pltpu.CompilerParams(vmem_limit_bytes=40 * 1024 * 1024),
        cost_estimate=pl.CostEstimate(flops=flops, bytes_accessed=moved, transcendentals=0),
    )(*args)


def exchange(block, axis, members):
    rows = block.shape[0] // members
    parted = block.reshape(members, rows, block.shape[1])
    return lax.all_to_all(parted, axis, 0, 0, tiled=True).reshape(block.shape)


def local(q_gate, k_gate, values, filter_raw, grad_out):
    shards = lax.axis_size("seq")
    members = lax.axis_size("chan")
    total = SIDE * SIDE
    into, back, ahead, behind, twist = (
        jnp.asarray(t) for t in tables(shards, total ** (-0.5) / total)
    )
    pitch = 80
    rows = 32 * shards
    packed = call(
        functools.partial(pack_kernel, shards, pitch),
        [(pitch * shards, SIDE)],
        (k_gate, values, grad_out, q_gate, filter_raw),
        "pack",
    )[0]
    spread = exchange(packed, "seq", shards)
    heavy = 6 * 10**9
    conv_out, gated_spec, filt_spec = call(
        functools.partial(conv_kernel, shards, pitch),
        [(rows, SIDE), (8 * SIDE, 2 * SIDE), (GROUP * SIDE, 2 * SIDE)],
        (spread, into, back, ahead, behind, twist),
        "conv",
        heavy,
    )
    conv = exchange(conv_out, "seq", shards)
    corr_out, grad_spec = call(
        functools.partial(corr_kernel, shards, pitch),
        [(8 * 2 * shards, SIDE), (8 * SIDE, 2 * SIDE)],
        (spread, gated_spec, into, back, ahead, behind, twist),
        "corr",
        heavy,
    )
    back_out = call(
        functools.partial(back_kernel, shards),
        [(rows, SIDE)],
        (grad_spec, filt_spec, back, behind, twist),
        "back",
        heavy,
    )[0]
    chunk = 2 * shards
    me = lax.axis_index("chan")
    parts = corr_out.reshape(members, chunk, SIDE)
    ring = [[(i, (i + d) % members) for i in range(members)] for d in range(members)]
    pieces = [lax.dynamic_index_in_dim(parts, me, 0, keepdims=False)]
    for d in range(1, members):
        piece = lax.dynamic_index_in_dim(parts, (me + d) % members, 0, keepdims=False)
        pieces.append(lax.ppermute(piece, "chan", ring[d]))
    summed = functools.reduce(jnp.add, pieces)
    summed, conv = lax.optimization_barrier((summed, conv))
    placed = exchange(summed, "seq", shards)
    placed, back_out = lax.optimization_barrier((placed, back_out))
    grad_gated = exchange(back_out, "seq", shards)
    wide = lax.all_to_all(
        jnp.broadcast_to(placed, (members, chunk, SIDE)), "chan", 0, 0, tiled=True
    ).reshape(members * chunk, SIDE)
    block = q_gate.shape
    grad_q = call(functools.partial(unpack_kernel, shards), [block], (conv, grad_out), "unpack_q")[0]
    grad_k, grad_v = call(
        functools.partial(unpack_kernel, shards),
        [block, block],
        (grad_gated, values, k_gate),
        "unpack_kv",
    )
    grad_filter = call(
        functools.partial(filter_kernel, shards), [filter_raw.shape], (wide,), "unpack_f"
    )[0]
    return grad_q, grad_k, grad_v, grad_filter


def solution(mesh):
    placed = (
        P("seq", "chan"),
        P("seq", "chan"),
        P("seq", "chan"),
        P("seq", None),
        P("seq", "chan"),
    )
    return jax.shard_map(
        local,
        mesh=mesh,
        in_specs=placed,
        out_specs=(P("seq", "chan"), P("seq", "chan"), P("seq", "chan"), P("seq", None)),
        check_vma=False,
    )
```

```python
import functools

import jax
import jax.numpy as jnp
import numpy as np
from jax import lax
from jax.experimental import pallas as pl
from jax.experimental.pallas import tpu as pltpu
from jax.sharding import Mesh
from jax.sharding import PartitionSpec as P


SIDE = 128
HALVES = 2
BLOCKS = 4
QUARTERS = 4
IN_ROWS = 17
OUT_ROWS = 20
BF = jnp.bfloat16
F32 = jnp.float32


def split_np(table):
    high = table.astype(np.float32).astype(BF)
    low = (table - high.astype(np.float64)).astype(np.float32).astype(BF)
    return high, low


def tables(shards, factor):
    total = SIDE * SIDE
    index = np.arange(SIDE)
    quarter, source = np.divmod(index, shards)
    first = source * QUARTERS + quarter
    coarse = 2.0 * np.pi * np.outer(index + 0.25, first) / SIDE
    high, low = split_np(np.concatenate([np.cos(coarse), -np.sin(coarse)], axis=0))
    into = np.concatenate([high, low, high], axis=1)
    high, low = split_np(np.concatenate([np.cos(coarse.T), -np.sin(coarse.T)], axis=1) * factor)
    back = np.concatenate([high, low, high], axis=1)
    fine = 2.0 * np.pi * (np.outer(index, index) % SIDE) / SIDE
    cos, sin = np.cos(fine), np.sin(fine)
    high, low = split_np(np.block([[cos, -sin], [sin, cos]]))
    ahead = np.concatenate([high, high, low], axis=0)
    high, low = split_np(np.block([[cos, sin], [-sin, cos]]))
    behind = np.concatenate([high, high, low], axis=0)
    turn = 2.0 * np.pi * np.outer(index + 0.25, index) / total
    twist = np.concatenate([np.cos(turn), np.sin(turn)], axis=1).astype(np.float32)
    return into, back, ahead, behind, twist


def halves(value):
    high = value.astype(BF)
    return high, (value - high.astype(F32)).astype(BF)


def dot(left, right):
    return jnp.dot(left, right, preferred_element_type=F32)


def transform(slabs, into, ahead, twist):
    high, low = halves(jnp.concatenate(slabs, axis=1))
    coarse = dot(into, jnp.concatenate([high, high, low], axis=0))
    cos, sin = twist[:, :SIDE], twist[:, SIDE:]
    rows = []
    for at in range(len(slabs)):
        real = coarse[:SIDE, at * SIDE : (at + 1) * SIDE]
        imag = coarse[SIDE:, at * SIDE : (at + 1) * SIDE]
        rows.append(
            jnp.concatenate([real * cos + imag * sin, imag * cos - real * sin], axis=1)
        )
    high, low = halves(jnp.concatenate(rows, axis=0))
    return dot(jnp.concatenate([high, low, high], axis=1), ahead)


def inverse(specs, back, behind, twist):
    high, low = halves(jnp.concatenate(specs, axis=0))
    fine = dot(jnp.concatenate([high, low, high], axis=1), behind)
    cos, sin = twist[:, :SIDE], twist[:, SIDE:]
    reals, imags = [], []
    for at in range(len(specs)):
        real = fine[at * SIDE : (at + 1) * SIDE, :SIDE]
        imag = fine[at * SIDE : (at + 1) * SIDE, SIDE:]
        reals.append(real * cos - imag * sin)
        imags.append(imag * cos + real * sin)
    turned = jnp.concatenate(
        [jnp.concatenate(reals, axis=1), jnp.concatenate(imags, axis=1)], axis=0
    )
    high, low = halves(turned)
    return dot(back, jnp.concatenate([high, high, low], axis=0))


def product(left, right):
    lr, li = left[:, :SIDE], left[:, SIDE:]
    rr, ri = right[:, :SIDE], right[:, SIDE:]
    return jnp.concatenate([lr * rr - li * ri, lr * ri + li * rr], axis=1)


def turned_product(left, right):
    lr, li = left[:, :SIDE], left[:, SIDE:]
    rr, ri = right[:, :SIDE], right[:, SIDE:]
    return jnp.concatenate([lr * rr + li * ri, lr * ri - li * rr], axis=1)


def gather_rows(ref, base, step, shards, pitch):
    return jnp.concatenate(
        [ref[pl.ds(base + q * step, shards, stride=pitch), :] for q in range(QUARTERS)], axis=0
    )


def pack_kernel(
    members, near_ref, k_hbm, v_hbm, g_hbm, q_hbm, f_hbm, out_ref,
    k_ref, v_ref, g_ref, q_ref, f_ref, sems,
):
    copies = []
    for q in range(QUARTERS):
        rows = pl.ds(q * SIDE, SIDE)
        pairs = ((k_hbm, k_ref), (v_hbm, v_ref), (g_hbm, g_ref), (q_hbm, q_ref))
        for at, (source, target) in enumerate(pairs):
            copy = pltpu.make_async_copy(source.at[rows], target.at[rows], sems.at[q * 4 + at])
            copy.start()
            copies.append(copy)
    start = pl.multiple_of(near_ref[0] * SIDE, SIDE)
    last = pltpu.make_async_copy(f_hbm.at[pl.ds(start, SIDE)], f_ref, sems.at[16])
    last.start()
    for q in range(QUARTERS):
        for at in range(4):
            copies[q * 4 + at].wait()
        rows = slice(q * SIDE, (q + 1) * SIDE)
        for h in range(HALVES):
            cols = slice(h * SIDE, (h + 1) * SIDE)
            at = h * QUARTERS + q
            out_ref[pl.ds(at, members, stride=IN_ROWS), :] = (
                k_ref[rows, cols] * v_ref[rows, cols]
            ).T
            out_ref[pl.ds(8 + at, members, stride=IN_ROWS), :] = (
                g_ref[rows, cols] * q_ref[rows, cols]
            ).T
    last.wait()
    out_ref[pl.ds(16, members, stride=IN_ROWS), :] = f_ref[...].T


def ahead_kernel(
    shards, in_ref, into_ref, back_ref, ahead_ref, behind_ref, twist_ref,
    corr_ref, gated_ref, grad_ref,
):
    into, ahead, twist = into_ref[...], ahead_ref[...], twist_ref[...]
    pitch = BLOCKS * IN_ROWS
    total = None
    for block in range(BLOCKS):
        specs = []
        for array, out_ref in enumerate((gated_ref, grad_ref)):
            slabs = [
                gather_rows(
                    in_ref, block * IN_ROWS + array * 8 + h * QUARTERS, 1, shards, pitch
                )
                for h in range(HALVES)
            ]
            spec = transform(slabs, into, ahead, twist)
            out_ref[pl.ds(block * 2 * SIDE, 2 * SIDE), :] = spec
            specs.append(spec)
        term = turned_product(*specs)
        term = term[:SIDE] + term[SIDE:]
        total = term if total is None else total + term
    corr_ref[...] = inverse([total], back_ref[...], behind_ref[...], twist)


def behind_kernel(
    shards, in_ref, gated_ref, grad_ref, into_ref, back_ref, ahead_ref, behind_ref, twist_ref,
    out_ref,
):
    twist, back, behind = twist_ref[...], back_ref[...], behind_ref[...]
    pitch = BLOCKS * OUT_ROWS
    slab = gather_rows(in_ref, 16, IN_ROWS, shards, BLOCKS * IN_ROWS)
    filt = transform([slab], into_ref[...], ahead_ref[...], twist)
    for block in range(BLOCKS):
        for array, spec_ref in enumerate((gated_ref, grad_ref)):
            combine = turned_product if array else product
            specs = [
                combine(filt, spec_ref[pl.ds((block * 2 + h) * SIDE, SIDE), :])
                for h in range(HALVES)
            ]
            result = inverse(specs, back, behind, twist)
            for h in range(HALVES):
                for q in range(QUARTERS):
                    at = block * OUT_ROWS + array * 8 + h * QUARTERS + q
                    out_ref[pl.ds(at, shards, stride=pitch), :] = result[
                        q * shards : (q + 1) * shards, h * SIDE : (h + 1) * SIDE
                    ]


def sum_kernel(shards, own_ref, other_ref, _, out_ref):
    total = own_ref[...] + other_ref[...]
    for block in range(BLOCKS):
        for q in range(QUARTERS):
            at = block * OUT_ROWS + 16 + q
            out_ref[pl.ds(at, shards, stride=BLOCKS * OUT_ROWS), :] = total[
                q * shards : (q + 1) * shards
            ]


def unpack_kernel(
    members, in_ref, g_ref, v_ref, k_ref, gq_hbm, gk_hbm, gv_hbm, gf_hbm,
    gq_ref, gk_ref, gv_ref, gf_ref, sems,
):
    copies = []
    for q in range(QUARTERS):
        rows = slice(q * SIDE, (q + 1) * SIDE)
        for h in range(HALVES):
            cols = slice(h * SIDE, (h + 1) * SIDE)
            at = h * QUARTERS + q
            conv = in_ref[pl.ds(at, members, stride=OUT_ROWS), :].T
            gq_ref[rows, cols] = conv * g_ref[rows, cols]
            back = in_ref[pl.ds(8 + at, members, stride=OUT_ROWS), :].T
            gk_ref[rows, cols] = back * v_ref[rows, cols]
            gv_ref[rows, cols] = back * k_ref[rows, cols]
        gf_ref[rows, :] = in_ref[pl.ds(16 + q, members, stride=OUT_ROWS), :].T
        pairs = ((gq_ref, gq_hbm), (gk_ref, gk_hbm), (gv_ref, gv_hbm), (gf_ref, gf_hbm))
        for at, (source, target) in enumerate(pairs):
            part = pl.ds(q * SIDE, SIDE)
            copy = pltpu.make_async_copy(source.at[part], target.at[part], sems.at[q * 4 + at])
            copy.start()
            copies.append(copy)
    for copy in copies:
        copy.wait()


VMEM = pl.BlockSpec(memory_space=pltpu.VMEM)
HBM = pl.BlockSpec(memory_space=pltpu.HBM)
SMEM = pl.BlockSpec(memory_space=pltpu.SMEM)
LIMIT = 24 * 1024 * 1024


def call(kernel, outs, args, name, ins=None, out_spec=VMEM, scratch=(), flops=0, aliases=None):
    moved = sum(4 * int(np.prod(shape)) for shape in outs)
    moved += sum(a.size * a.dtype.itemsize for a in args)
    return pl.pallas_call(
        kernel,
        out_shape=[jax.ShapeDtypeStruct(shape, F32) for shape in outs],
        in_specs=ins or [VMEM] * len(args),
        out_specs=[out_spec] * len(outs),
        scratch_shapes=list(scratch),
        input_output_aliases=aliases or {},
        name=name,
        compiler_params=pltpu.CompilerParams(vmem_limit_bytes=LIMIT),
        cost_estimate=pl.CostEstimate(flops=flops, bytes_accessed=moved, transcendentals=0),
    )(*args)


def exchange(block, inner):
    parted = block.reshape(block.shape[0] // int(np.prod(inner)), *inner, SIDE)
    return lax.all_to_all(parted, ("seq", "near"), 0, 0, tiled=True).reshape(block.shape)


def local(q_gate, k_gate, values, filter_raw, grad_out):
    shards = lax.axis_size("seq")
    members = shards * lax.axis_size("near")
    total = SIDE * SIDE
    into, back, ahead, behind, twist = (
        jnp.asarray(t) for t in tables(shards, total ** (-0.5) / total)
    )
    block = q_gate.shape
    wide = pltpu.VMEM(block, F32)
    near = lax.axis_index("near").astype(jnp.int32).reshape(1)
    packed = call(
        functools.partial(pack_kernel, members),
        [(IN_ROWS * members, SIDE)],
        (near, *(pltpu.with_memory_space_constraint(a, pltpu.HBM) for a in (k_gate, values, grad_out, q_gate, filter_raw))),
        "pack",
        ins=[SMEM] + [HBM] * 5,
        scratch=[wide] * 4 + [pltpu.VMEM((SIDE, SIDE), F32), pltpu.SemaphoreType.DMA((17,))],
    )[0]
    spread = exchange(packed, (17, 1))
    corr, gated_spec, grad_spec = call(
        functools.partial(ahead_kernel, shards),
        [(SIDE, SIDE), (8 * SIDE, 2 * SIDE), (8 * SIDE, 2 * SIDE)],
        (spread, into, back, ahead, behind, twist),
        "ahead",
        flops=10**9,
    )
    other = lax.ppermute(corr, "far", [(0, 1), (1, 0)])
    results = call(
        functools.partial(behind_kernel, shards),
        [(OUT_ROWS * members, SIDE)],
        (spread, gated_spec, grad_spec, into, back, ahead, behind, twist),
        "behind",
        flops=10**9,
    )[0]
    results = call(
        functools.partial(sum_kernel, shards),
        [(OUT_ROWS * members, SIDE)],
        (corr, other, results),
        "sum",
        ins=[VMEM] * 3,
        aliases={2: 0},
    )[0]
    placed = exchange(results, (5, 4))
    grad_q, grad_k, grad_v, grad_filter = call(
        functools.partial(unpack_kernel, members),
        [block, block, block, filter_raw.shape],
        (placed, grad_out, values, k_gate),
        "unpack",
        out_spec=HBM,
        scratch=[wide] * 3 + [pltpu.VMEM(filter_raw.shape, F32), pltpu.SemaphoreType.DMA((16,))],
    )
    return grad_q, grad_k, grad_v, grad_filter


def solution(mesh):
    shards, groups = mesh.devices.shape
    parted = Mesh(
        mesh.devices.reshape(shards, groups // BLOCKS, BLOCKS), ("seq", "far", "near")
    )
    whole, filters = P("seq", ("far", "near")), P("seq", None)
    return jax.shard_map(
        local,
        mesh=parted,
        in_specs=(whole, whole, whole, filters, whole),
        out_specs=(whole, whole, whole, filters),
        check_vma=False,
    )
```

```python
import functools

import jax
import jax.numpy as jnp
import numpy as np
from jax import lax
from jax.experimental import pallas as pl
from jax.experimental.pallas import tpu as pltpu
from jax.sharding import Mesh
from jax.sharding import PartitionSpec as P


SIDE = 128
HALVES = 2
BLOCKS = 4
QUARTERS = 4
IN_ROWS = 17
OUT_ROWS = 20
BF = jnp.bfloat16
F32 = jnp.float32


def split_np(table):
    high = table.astype(np.float32).astype(BF)
    low = (table - high.astype(np.float64)).astype(np.float32).astype(BF)
    return high, low


def tables(shards, factor):
    total = SIDE * SIDE
    index = np.arange(SIDE)
    quarter, source = np.divmod(index, shards)
    first = source * QUARTERS + quarter
    coarse = 2.0 * np.pi * np.outer(index + 0.25, first) / SIDE
    high, low = split_np(np.concatenate([np.cos(coarse), -np.sin(coarse)], axis=0))
    into = np.concatenate([high, low, high], axis=1)
    high, low = split_np(np.concatenate([np.cos(coarse.T), -np.sin(coarse.T)], axis=1) * factor)
    back = np.concatenate([high, low], axis=0)
    fine = 2.0 * np.pi * (np.outer(index, index) % SIDE) / SIDE
    cos, sin = np.cos(fine), np.sin(fine)
    high, low = split_np(np.block([[cos, -sin], [sin, cos]]))
    ahead = np.concatenate([high, high, low], axis=0)
    high, low = split_np(np.block([[cos, sin], [-sin, cos]]))
    behind = np.concatenate([high, high, low], axis=0)
    turn = 2.0 * np.pi * np.outer(index + 0.25, index) / total
    twist = np.concatenate([np.cos(turn), np.sin(turn)], axis=1).astype(np.float32)
    return into, back, ahead, behind, twist


def halves(value):
    high = value.astype(BF)
    return high, (value - high.astype(F32)).astype(BF)


def dot(left, right):
    return jnp.dot(left, right, preferred_element_type=F32)


def coarse_stage(slabs, into, twist, high_ref, low_ref, row):
    high, low = halves(jnp.concatenate(slabs, axis=1))
    coarse = dot(into, jnp.concatenate([high, high, low], axis=0))
    cos, sin = twist[:, :SIDE], twist[:, SIDE:]
    for at in range(len(slabs)):
        real = coarse[:SIDE, at * SIDE : (at + 1) * SIDE]
        imag = coarse[SIDE:, at * SIDE : (at + 1) * SIDE]
        store_halves(
            jnp.concatenate([real * cos + imag * sin, imag * cos - real * sin], axis=1),
            high_ref, low_ref, row + at * SIDE,
        )


def store_halves(value, high_ref, low_ref, row):
    high, low = halves(value)
    rows = slice(row, row + value.shape[0])
    high_ref[rows, :] = high
    low_ref[rows, :] = low


def fine_stage(high_ref, low_ref, row, count, matrix, pieces=2):
    size = count // pieces
    results = []
    for at in range(pieces):
        rows = slice(row + at * size, row + (at + 1) * size)
        high, low = high_ref[rows, :], low_ref[rows, :]
        results.append(dot(jnp.concatenate([high, low, high], axis=1), matrix))
    return results


def last_stage(fine, back, twist):
    cos, sin = twist[:, :SIDE], twist[:, SIDE:]
    split = []
    for at in range(0, len(fine), 2):
        reals, imags = [], []
        for slab in fine[at : at + 2]:
            real, imag = slab[:, :SIDE], slab[:, SIDE:]
            reals.append(real * cos - imag * sin)
            imags.append(imag * cos + real * sin)
        turned = jnp.concatenate(
            [jnp.concatenate(reals, axis=1), jnp.concatenate(imags, axis=1)], axis=0
        )
        split.append(halves(turned))
    both = [dot(back, high) for high, _ in split]
    rest = [dot(back[:SIDE], low) for _, low in split]
    return [b[:SIDE] + b[SIDE:] + r for b, r in zip(both, rest)]


def slabs_of(parts):
    return [part[at : at + SIDE] for part in parts for at in range(0, part.shape[0], SIDE)]


def product(left, right):
    lr, li = left[:, :SIDE], left[:, SIDE:]
    rr, ri = right[:, :SIDE], right[:, SIDE:]
    return jnp.concatenate([lr * rr - li * ri, lr * ri + li * rr], axis=1)


def turned_product(left, right):
    lr, li = left[:, :SIDE], left[:, SIDE:]
    rr, ri = right[:, :SIDE], right[:, SIDE:]
    return jnp.concatenate([lr * rr + li * ri, lr * ri - li * rr], axis=1)


def gather_rows(ref, base, step, shards, pitch):
    return jnp.concatenate(
        [ref[pl.ds(base + q * step, shards, stride=pitch), :] for q in range(QUARTERS)], axis=0
    )


def pack_kernel(
    members, near_ref, k_hbm, v_hbm, g_hbm, q_hbm, f_hbm, out_ref,
    k_ref, v_ref, g_ref, q_ref, f_ref, sems,
):
    copies = []
    for q in range(QUARTERS):
        rows = pl.ds(q * SIDE, SIDE)
        pairs = ((k_hbm, k_ref), (v_hbm, v_ref), (g_hbm, g_ref), (q_hbm, q_ref))
        for at, (source, target) in enumerate(pairs):
            copy = pltpu.make_async_copy(source.at[rows], target.at[rows], sems.at[q * 4 + at])
            copy.start()
            copies.append(copy)
        if q == 0:
            start = pl.multiple_of(near_ref[0] * SIDE, SIDE)
            own = pltpu.make_async_copy(f_hbm.at[pl.ds(start, SIDE)], f_ref, sems.at[16])
            own.start()
    for q in range(QUARTERS):
        rows = slice(q * SIDE, (q + 1) * SIDE)
        for array, (left, right) in enumerate(((k_ref, v_ref), (g_ref, q_ref))):
            copies[q * 4 + array * 2].wait()
            copies[q * 4 + array * 2 + 1].wait()
            for h in range(HALVES):
                cols = slice(h * SIDE, (h + 1) * SIDE)
                at = array * 8 + h * QUARTERS + q
                out_ref[pl.ds(at, members, stride=IN_ROWS), :] = (
                    left[rows, cols] * right[rows, cols]
                ).T
        if q == 0:
            own.wait()
            out_ref[pl.ds(16, members, stride=IN_ROWS), :] = f_ref[...].T


def ahead_kernel(
    shards, in_ref, into_ref, back_ref, ahead_ref, behind_ref, twist_ref,
    corr_ref, gated_ref, grad_ref, high_ref, low_ref,
):
    into, twist = into_ref[...], twist_ref[...]
    pitch = BLOCKS * IN_ROWS
    span = BLOCKS * HALVES * SIDE
    half = span // 2
    total = None
    for part in range(2):
        for array in range(2):
            slabs = [
                gather_rows(
                    in_ref, block * IN_ROWS + array * 8 + h * QUARTERS, 1, shards, pitch
                )
                for block in (part * 2, part * 2 + 1)
                for h in range(HALVES)
            ]
            coarse_stage(slabs, into, twist, high_ref, low_ref, part * span + array * half)
    for part in range(2):
        both = fine_stage(high_ref, low_ref, part * span, span, ahead_ref[...], 1)[0]
        both = (both[:half], both[half:])
        rows = slice(part * half, (part + 1) * half)
        gated_ref[rows, :] = both[0]
        grad_ref[rows, :] = both[1]
        for at in range(0, half, SIDE):
            term = turned_product(both[0][at : at + SIDE], both[1][at : at + SIDE])
            total = term if total is None else total + term
    store_halves(total, high_ref, low_ref, 2 * span)
    fine = fine_stage(high_ref, low_ref, 2 * span, SIDE, behind_ref[...], 1)
    corr_ref[...] = last_stage([jnp.concatenate(fine, axis=0)], back_ref[...], twist)[0]


def behind_kernel(
    shards, in_ref, gated_ref, grad_ref, into_ref, back_ref, ahead_ref, behind_ref, twist_ref,
    out_ref, high_ref, low_ref,
):
    twist, back = twist_ref[...], back_ref[...]
    pitch = BLOCKS * OUT_ROWS
    group = 2 * HALVES * SIDE
    spare = BLOCKS * group
    slab = gather_rows(in_ref, 16, IN_ROWS, shards, BLOCKS * IN_ROWS)
    coarse_stage([slab], into_ref[...], twist, high_ref, low_ref, spare)
    filt = jnp.concatenate(fine_stage(high_ref, low_ref, spare, SIDE, ahead_ref[...]), axis=0)
    for block in range(BLOCKS):
        for array, spec_ref in enumerate((gated_ref, grad_ref)):
            combine = turned_product if array else product
            for h in range(HALVES):
                spec = spec_ref[pl.ds((block * 2 + h) * SIDE, SIDE), :]
                row = block * group + (array * HALVES + h) * SIDE
                store_halves(combine(filt, spec), high_ref, low_ref, row)
    for part in range(2):
        fine = slabs_of(
            fine_stage(high_ref, low_ref, part * 2 * group, 2 * group, behind_ref[...])
        )
        for near in range(2):
            block = part * 2 + near
            results = last_stage(fine[near * 4 : near * 4 + 4], back, twist)
            for at in range(2 * HALVES):
                column = at % 2 * SIDE
                for q in range(QUARTERS):
                    row = block * OUT_ROWS + at * QUARTERS + q
                    out_ref[pl.ds(row, shards, stride=pitch), :] = results[at // 2][
                        q * shards : (q + 1) * shards, column : column + SIDE
                    ]


def sum_kernel(shards, own_ref, other_ref, _, out_ref):
    total = own_ref[...] + other_ref[...]
    for block in range(BLOCKS):
        for q in range(QUARTERS):
            at = block * OUT_ROWS + 16 + q
            out_ref[pl.ds(at, shards, stride=BLOCKS * OUT_ROWS), :] = total[
                q * shards : (q + 1) * shards
            ]


def unpack_kernel(
    members, in_ref, g_ref, v_ref, k_ref, gq_hbm, gk_hbm, gv_hbm, gf_hbm,
    gq_ref, gk_ref, gv_ref, gf_ref, sems,
):
    copies = []
    for q in range(QUARTERS):
        rows = slice(q * SIDE, (q + 1) * SIDE)
        for h in range(HALVES):
            cols = slice(h * SIDE, (h + 1) * SIDE)
            at = h * QUARTERS + q
            conv = in_ref[pl.ds(at, members, stride=OUT_ROWS), :].T
            gq_ref[rows, cols] = conv * g_ref[rows, cols]
            back = in_ref[pl.ds(8 + at, members, stride=OUT_ROWS), :].T
            gk_ref[rows, cols] = back * v_ref[rows, cols]
            gv_ref[rows, cols] = back * k_ref[rows, cols]
        gf_ref[rows, :] = in_ref[pl.ds(16 + q, members, stride=OUT_ROWS), :].T
        pairs = ((gq_ref, gq_hbm), (gk_ref, gk_hbm), (gv_ref, gv_hbm), (gf_ref, gf_hbm))
        for at, (source, target) in enumerate(pairs):
            part = pl.ds(q * SIDE, SIDE)
            copy = pltpu.make_async_copy(source.at[part], target.at[part], sems.at[q * 4 + at])
            copy.start()
            copies.append(copy)
    for copy in copies:
        copy.wait()


VMEM = pl.BlockSpec(memory_space=pltpu.VMEM)
HBM = pl.BlockSpec(memory_space=pltpu.HBM)
SMEM = pl.BlockSpec(memory_space=pltpu.SMEM)
LIMIT = 24 * 1024 * 1024


def call(kernel, outs, args, name, ins=None, out_spec=VMEM, scratch=(), flops=0, aliases=None):
    moved = sum(4 * int(np.prod(shape)) for shape in outs)
    moved += sum(a.size * a.dtype.itemsize for a in args)
    return pl.pallas_call(
        kernel,
        out_shape=[jax.ShapeDtypeStruct(shape, F32) for shape in outs],
        in_specs=ins or [VMEM] * len(args),
        out_specs=[out_spec] * len(outs),
        scratch_shapes=list(scratch),
        input_output_aliases=aliases or {},
        name=name,
        compiler_params=pltpu.CompilerParams(vmem_limit_bytes=LIMIT),
        cost_estimate=pl.CostEstimate(flops=flops, bytes_accessed=moved, transcendentals=0),
    )(*args)


def exchange(block, inner):
    parted = block.reshape(block.shape[0] // int(np.prod(inner)), *inner, SIDE)
    return lax.all_to_all(parted, ("seq", "far", "mid"), 0, 0, tiled=True).reshape(block.shape)


def local(q_gate, k_gate, values, filter_raw, grad_out):
    shards = lax.axis_size("seq")
    members = shards * BLOCKS
    total = SIDE * SIDE
    into, back, ahead, behind, twist = (
        jnp.asarray(t) for t in tables(shards, total ** (-0.5) / total)
    )
    block = q_gate.shape
    wide = pltpu.VMEM(block, F32)
    split = [pltpu.VMEM((17 * SIDE, 2 * SIDE), BF)] * 2
    near = lax.axis_index(("far", "mid")).astype(jnp.int32).reshape(1)
    packed = call(
        functools.partial(pack_kernel, members),
        [(IN_ROWS * members, SIDE)],
        (near, *(pltpu.with_memory_space_constraint(a, pltpu.HBM) for a in (k_gate, values, grad_out, q_gate, filter_raw))),
        "pack",
        ins=[SMEM] + [HBM] * 5,
        scratch=[wide] * 4 + [pltpu.VMEM((SIDE, SIDE), F32), pltpu.SemaphoreType.DMA((17,))],
    )[0]
    spread = exchange(packed, (17, 1))
    corr, gated_spec, grad_spec = call(
        functools.partial(ahead_kernel, shards),
        [(SIDE, SIDE), (8 * SIDE, 2 * SIDE), (8 * SIDE, 2 * SIDE)],
        (spread, into, back, ahead, behind, twist),
        "ahead",
        scratch=split,
        flops=10**9,
    )
    other = lax.ppermute(corr, "pair", [(0, 1), (1, 0)])
    results = call(
        functools.partial(behind_kernel, shards),
        [(OUT_ROWS * members, SIDE)],
        (spread, gated_spec, grad_spec, into, back, ahead, behind, twist),
        "behind",
        scratch=split,
        flops=10**9,
    )[0]
    results = call(
        functools.partial(sum_kernel, shards),
        [(OUT_ROWS * members, SIDE)],
        (corr, other, results),
        "sum",
        ins=[VMEM] * 3,
        aliases={2: 0},
    )[0]
    placed = exchange(results, (5, 4))
    grad_q, grad_k, grad_v, grad_filter = call(
        functools.partial(unpack_kernel, members),
        [block, block, block, filter_raw.shape],
        (placed, grad_out, values, k_gate),
        "unpack",
        out_spec=HBM,
        scratch=[wide] * 3 + [pltpu.VMEM(filter_raw.shape, F32), pltpu.SemaphoreType.DMA((16,))],
    )
    return grad_q, grad_k, grad_v, grad_filter


def solution(mesh):
    shards, groups = mesh.devices.shape
    parted = Mesh(
        mesh.devices.reshape(shards, 2, groups // 4, 2), ("seq", "far", "mid", "pair")
    )
    whole, filters = P("seq", ("far", "mid", "pair")), P("seq", None)
    return jax.shard_map(
        local,
        mesh=parted,
        in_specs=(whole, whole, whole, filters, whole),
        out_specs=(whole, whole, whole, filters),
        check_vma=False,
    )
```

```python
import functools

import jax
import jax.numpy as jnp
import numpy as np
from jax import lax
from jax.experimental import pallas as pl
from jax.experimental.pallas import tpu as pltpu
from jax.sharding import Mesh
from jax.sharding import PartitionSpec as P


SIDE = 128
HALVES = 2
BLOCKS = 4
QUARTERS = 4
IN_ROWS = 17
OUT_ROWS = 20
BF = jnp.bfloat16
F32 = jnp.float32


def split_np(table):
    high = table.astype(np.float32).astype(BF)
    low = (table - high.astype(np.float64)).astype(np.float32).astype(BF)
    return high, low


def tables(shards, factor):
    total = SIDE * SIDE
    index = np.arange(SIDE)
    quarter, source = np.divmod(index, shards)
    first = source * QUARTERS + quarter
    coarse = 2.0 * np.pi * np.outer(index + 0.25, first) / SIDE
    high, low = split_np(np.concatenate([np.cos(coarse), -np.sin(coarse)], axis=0))
    into = np.concatenate([high, low, high], axis=1)
    high, low = split_np(np.concatenate([np.cos(coarse.T), -np.sin(coarse.T)], axis=1) * factor)
    back = np.concatenate([high, low], axis=0)
    fine = 2.0 * np.pi * (np.outer(index, index) % SIDE) / SIDE
    cos, sin = np.cos(fine), np.sin(fine)
    high, low = split_np(np.block([[cos, -sin], [sin, cos]]))
    ahead = np.concatenate([high, high, low], axis=0)
    high, low = split_np(np.block([[cos, sin], [-sin, cos]]))
    behind = np.concatenate([high, high, low], axis=0)
    turn = 2.0 * np.pi * np.outer(index + 0.25, index) / total
    twist = np.concatenate([np.cos(turn), np.sin(turn)], axis=1).astype(np.float32)
    return into, back, ahead, behind, twist


def halves(value):
    high = value.astype(BF)
    return high, (value - high.astype(F32)).astype(BF)


def dot(left, right):
    return jnp.dot(left, right, preferred_element_type=F32)


def coarse_stage(slabs, into, twist, high_ref, low_ref, row):
    high, low = halves(jnp.concatenate(slabs, axis=1))
    coarse = dot(into, jnp.concatenate([high, high, low], axis=0))
    cos, sin = twist[:, :SIDE], twist[:, SIDE:]
    for at in range(len(slabs)):
        real = coarse[:SIDE, at * SIDE : (at + 1) * SIDE]
        imag = coarse[SIDE:, at * SIDE : (at + 1) * SIDE]
        store_halves(
            jnp.concatenate([real * cos + imag * sin, imag * cos - real * sin], axis=1),
            high_ref, low_ref, row + at * SIDE,
        )


def store_halves(value, high_ref, low_ref, row):
    high, low = halves(value)
    rows = slice(row, row + value.shape[0])
    high_ref[rows, :] = high
    low_ref[rows, :] = low


def fine_stage(high_ref, low_ref, row, count, matrix, pieces=2):
    size = count // pieces
    results = []
    for at in range(pieces):
        rows = slice(row + at * size, row + (at + 1) * size)
        high, low = high_ref[rows, :], low_ref[rows, :]
        results.append(dot(jnp.concatenate([high, low, high], axis=1), matrix))
    return results


def last_stage(fine, back, twist):
    cos, sin = twist[:, :SIDE], twist[:, SIDE:]
    split = []
    for at in range(0, len(fine), 2):
        reals, imags = [], []
        for slab in fine[at : at + 2]:
            real, imag = slab[:, :SIDE], slab[:, SIDE:]
            reals.append(real * cos - imag * sin)
            imags.append(imag * cos + real * sin)
        turned = jnp.concatenate(
            [jnp.concatenate(reals, axis=1), jnp.concatenate(imags, axis=1)], axis=0
        )
        split.append(halves(turned))
    both = [dot(back, high) for high, _ in split]
    rest = [dot(back[:SIDE], low) for _, low in split]
    return [b[:SIDE] + b[SIDE:] + r for b, r in zip(both, rest)]


def slabs_of(parts):
    return [part[at : at + SIDE] for part in parts for at in range(0, part.shape[0], SIDE)]


def product(left, right):
    lr, li = left[:, :SIDE], left[:, SIDE:]
    rr, ri = right[:, :SIDE], right[:, SIDE:]
    return jnp.concatenate([lr * rr - li * ri, lr * ri + li * rr], axis=1)


def turned_product(left, right):
    lr, li = left[:, :SIDE], left[:, SIDE:]
    rr, ri = right[:, :SIDE], right[:, SIDE:]
    return jnp.concatenate([lr * rr + li * ri, lr * ri - li * rr], axis=1)


def gather_rows(ref, base, step, shards, pitch):
    return jnp.concatenate(
        [ref[pl.ds(base + q * step, shards, stride=pitch), :] for q in range(QUARTERS)], axis=0
    )


def pack_kernel(
    members, near_ref, k_hbm, v_hbm, g_hbm, q_hbm, f_hbm, out_ref,
    k_ref, v_ref, g_ref, q_ref, f_ref, sems,
):
    copies = []
    for q in range(QUARTERS):
        rows = pl.ds(q * SIDE, SIDE)
        pairs = ((k_hbm, k_ref), (v_hbm, v_ref), (g_hbm, g_ref), (q_hbm, q_ref))
        for at, (source, target) in enumerate(pairs):
            copy = pltpu.make_async_copy(source.at[rows], target.at[rows], sems.at[q * 4 + at])
            copy.start()
            copies.append(copy)
        if q == 0:
            start = pl.multiple_of(near_ref[0] * SIDE, SIDE)
            own = pltpu.make_async_copy(f_hbm.at[pl.ds(start, SIDE)], f_ref, sems.at[16])
            own.start()
    for q in range(QUARTERS):
        rows = slice(q * SIDE, (q + 1) * SIDE)
        for array, (left, right) in enumerate(((k_ref, v_ref), (g_ref, q_ref))):
            copies[q * 4 + array * 2].wait()
            copies[q * 4 + array * 2 + 1].wait()
            for h in range(HALVES):
                cols = slice(h * SIDE, (h + 1) * SIDE)
                at = array * 8 + h * QUARTERS + q
                out_ref[pl.ds(at, members, stride=IN_ROWS), :] = (
                    left[rows, cols] * right[rows, cols]
                ).T
        if q == 0:
            own.wait()
            out_ref[pl.ds(16, members, stride=IN_ROWS), :] = f_ref[...].T


def ahead_kernel(
    shards, in_ref, into_ref, back_ref, ahead_ref, behind_ref, twist_ref,
    corr_ref, gated_ref, grad_ref, high_ref, low_ref,
):
    into, twist = into_ref[...], twist_ref[...]
    pitch = BLOCKS * IN_ROWS
    span = BLOCKS * HALVES * SIDE
    half = span // 2
    total = None
    for part in range(2):
        for array in range(2):
            slabs = [
                gather_rows(
                    in_ref, block * IN_ROWS + array * 8 + h * QUARTERS, 1, shards, pitch
                )
                for block in (part * 2, part * 2 + 1)
                for h in range(HALVES)
            ]
            coarse_stage(slabs, into, twist, high_ref, low_ref, part * span + array * half)
    for part in range(2):
        both = fine_stage(high_ref, low_ref, part * span, span, ahead_ref[...], 1)[0]
        both = (both[:half], both[half:])
        rows = slice(part * half, (part + 1) * half)
        gated_ref[rows, :] = both[0]
        grad_ref[rows, :] = both[1]
        for at in range(0, half, SIDE):
            term = turned_product(both[0][at : at + SIDE], both[1][at : at + SIDE])
            total = term if total is None else total + term
    store_halves(total, high_ref, low_ref, 2 * span)
    fine = fine_stage(high_ref, low_ref, 2 * span, SIDE, behind_ref[...], 1)
    corr_ref[...] = last_stage([jnp.concatenate(fine, axis=0)], back_ref[...], twist)[0]


def behind_kernel(
    shards, in_ref, gated_ref, grad_ref, into_ref, back_ref, ahead_ref, behind_ref, twist_ref,
    out_ref, high_ref, low_ref,
):
    twist, back = twist_ref[...], back_ref[...]
    pitch = BLOCKS * OUT_ROWS
    group = 2 * HALVES * SIDE
    spare = BLOCKS * group
    slab = gather_rows(in_ref, 16, IN_ROWS, shards, BLOCKS * IN_ROWS)
    coarse_stage([slab], into_ref[...], twist, high_ref, low_ref, spare)
    filt = jnp.concatenate(fine_stage(high_ref, low_ref, spare, SIDE, ahead_ref[...]), axis=0)
    for block in range(BLOCKS):
        for array, spec_ref in enumerate((gated_ref, grad_ref)):
            combine = turned_product if array else product
            for h in range(HALVES):
                spec = spec_ref[pl.ds((block * 2 + h) * SIDE, SIDE), :]
                row = block * group + (array * HALVES + h) * SIDE
                store_halves(combine(filt, spec), high_ref, low_ref, row)
    for part in range(2):
        fine = slabs_of(
            fine_stage(high_ref, low_ref, part * 2 * group, 2 * group, behind_ref[...])
        )
        for near in range(2):
            block = part * 2 + near
            results = last_stage(fine[near * 4 : near * 4 + 4], back, twist)
            for at in range(2 * HALVES):
                column = at % 2 * SIDE
                for q in range(QUARTERS):
                    row = block * OUT_ROWS + at * QUARTERS + q
                    out_ref[pl.ds(row, shards, stride=pitch), :] = results[at // 2][
                        q * shards : (q + 1) * shards, column : column + SIDE
                    ]


def sum_kernel(shards, own_ref, other_ref, _, out_ref):
    total = own_ref[...] + other_ref[...]
    for block in range(BLOCKS):
        for q in range(QUARTERS):
            at = block * OUT_ROWS + 16 + q
            out_ref[pl.ds(at, shards, stride=BLOCKS * OUT_ROWS), :] = total[
                q * shards : (q + 1) * shards
            ]


def unpack_kernel(
    members, in_ref, g_ref, v_ref, k_ref, gq_hbm, gk_hbm, gv_hbm, gf_hbm,
    gq_ref, gk_ref, gv_ref, gf_ref, sems,
):
    copies = []
    for q in range(QUARTERS):
        rows = slice(q * SIDE, (q + 1) * SIDE)
        for h in range(HALVES):
            cols = slice(h * SIDE, (h + 1) * SIDE)
            at = h * QUARTERS + q
            conv = in_ref[pl.ds(at, members, stride=OUT_ROWS), :].T
            gq_ref[rows, cols] = conv * g_ref[rows, cols]
            back = in_ref[pl.ds(8 + at, members, stride=OUT_ROWS), :].T
            gk_ref[rows, cols] = back * v_ref[rows, cols]
            gv_ref[rows, cols] = back * k_ref[rows, cols]
        gf_ref[rows, :] = in_ref[pl.ds(16 + q, members, stride=OUT_ROWS), :].T
        pairs = ((gq_ref, gq_hbm), (gk_ref, gk_hbm), (gv_ref, gv_hbm), (gf_ref, gf_hbm))
        for at, (source, target) in enumerate(pairs):
            part = pl.ds(q * SIDE, SIDE)
            copy = pltpu.make_async_copy(source.at[part], target.at[part], sems.at[q * 4 + at])
            copy.start()
            copies.append(copy)
    for copy in copies:
        copy.wait()


VMEM = pl.BlockSpec(memory_space=pltpu.VMEM)
HBM = pl.BlockSpec(memory_space=pltpu.HBM)
SMEM = pl.BlockSpec(memory_space=pltpu.SMEM)
LIMIT = 24 * 1024 * 1024


def call(kernel, outs, args, name, ins=None, out_spec=VMEM, scratch=(), flops=0, aliases=None):
    moved = sum(4 * int(np.prod(shape)) for shape in outs)
    moved += sum(a.size * a.dtype.itemsize for a in args)
    return pl.pallas_call(
        kernel,
        out_shape=[jax.ShapeDtypeStruct(shape, F32) for shape in outs],
        in_specs=ins or [VMEM] * len(args),
        out_specs=[out_spec] * len(outs),
        scratch_shapes=list(scratch),
        input_output_aliases=aliases or {},
        name=name,
        compiler_params=pltpu.CompilerParams(vmem_limit_bytes=LIMIT),
        cost_estimate=pl.CostEstimate(flops=flops, bytes_accessed=moved, transcendentals=0),
    )(*args)


def exchange(block, inner):
    parted = block.reshape(block.shape[0] // int(np.prod(inner)), *inner, SIDE)
    return lax.all_to_all(parted, ("seq", "near"), 0, 0, tiled=True).reshape(block.shape)


def local(q_gate, k_gate, values, filter_raw, grad_out):
    shards = lax.axis_size("seq")
    members = shards * lax.axis_size("near")
    total = SIDE * SIDE
    into, back, ahead, behind, twist = (
        jnp.asarray(t) for t in tables(shards, total ** (-0.5) / total)
    )
    block = q_gate.shape
    wide = pltpu.VMEM(block, F32)
    split = [pltpu.VMEM((17 * SIDE, 2 * SIDE), BF)] * 2
    near = lax.axis_index("near").astype(jnp.int32).reshape(1)
    packed = call(
        functools.partial(pack_kernel, members),
        [(IN_ROWS * members, SIDE)],
        (near, *(pltpu.with_memory_space_constraint(a, pltpu.HBM) for a in (k_gate, values, grad_out, q_gate, filter_raw))),
        "pack",
        ins=[SMEM] + [HBM] * 5,
        scratch=[wide] * 4 + [pltpu.VMEM((SIDE, SIDE), F32), pltpu.SemaphoreType.DMA((17,))],
    )[0]
    spread = exchange(packed, (17, 1))
    corr, gated_spec, grad_spec = call(
        functools.partial(ahead_kernel, shards),
        [(SIDE, SIDE), (8 * SIDE, 2 * SIDE), (8 * SIDE, 2 * SIDE)],
        (spread, into, back, ahead, behind, twist),
        "ahead",
        scratch=split,
        flops=10**9,
    )
    other = lax.ppermute(corr, "far", [(0, 1), (1, 0)])
    results = call(
        functools.partial(behind_kernel, shards),
        [(OUT_ROWS * members, SIDE)],
        (spread, gated_spec, grad_spec, into, back, ahead, behind, twist),
        "behind",
        scratch=split,
        flops=10**9,
    )[0]
    results = call(
        functools.partial(sum_kernel, shards),
        [(OUT_ROWS * members, SIDE)],
        (corr, other, results),
        "sum",
        ins=[VMEM] * 3,
        aliases={2: 0},
    )[0]
    placed = exchange(results, (5, 4))
    grad_q, grad_k, grad_v, grad_filter = call(
        functools.partial(unpack_kernel, members),
        [block, block, block, filter_raw.shape],
        (placed, grad_out, values, k_gate),
        "unpack",
        out_spec=HBM,
        scratch=[wide] * 3 + [pltpu.VMEM(filter_raw.shape, F32), pltpu.SemaphoreType.DMA((16,))],
    )
    return grad_q, grad_k, grad_v, grad_filter


def solution(mesh):
    shards, groups = mesh.devices.shape
    parted = Mesh(
        mesh.devices.reshape(shards, groups // BLOCKS, BLOCKS), ("seq", "far", "near")
    )
    whole, filters = P("seq", ("far", "near")), P("seq", None)
    return jax.shard_map(
        local,
        mesh=parted,
        in_specs=(whole, whole, whole, filters, whole),
        out_specs=(whole, whole, whole, filters),
        check_vma=False,
    )
```

```python
import functools

import jax
import jax.numpy as jnp
import numpy as np
from jax import lax
from jax.experimental import pallas as pl
from jax.experimental.pallas import tpu as pltpu
from jax.sharding import Mesh
from jax.sharding import PartitionSpec as P


SIDE = 128
HALVES = 2
BLOCKS = 4
QUARTERS = 4
IN_ROWS = 17
OUT_ROWS = 20
BF = jnp.bfloat16
F32 = jnp.float32


def split_np(table):
    high = table.astype(np.float32).astype(BF)
    low = (table - high.astype(np.float64)).astype(np.float32).astype(BF)
    return high, low


def tables(shards, factor):
    total = SIDE * SIDE
    index = np.arange(SIDE)
    quarter, source = np.divmod(index, shards)
    first = source * QUARTERS + quarter
    coarse = 2.0 * np.pi * np.outer(index + 0.25, first) / SIDE
    high, low = split_np(np.concatenate([np.cos(coarse), -np.sin(coarse)], axis=0))
    into = np.concatenate([high, low, high], axis=1)
    high, low = split_np(np.concatenate([np.cos(coarse.T), -np.sin(coarse.T)], axis=1) * factor)
    back = np.concatenate([high, low], axis=0)
    fine = 2.0 * np.pi * (np.outer(index, index) % SIDE) / SIDE
    cos, sin = np.cos(fine), np.sin(fine)
    high, low = split_np(np.block([[cos, -sin], [sin, cos]]))
    ahead = np.concatenate([high, high, low], axis=0)
    high, low = split_np(np.block([[cos, sin], [-sin, cos]]))
    behind = np.concatenate([high, high, low], axis=0)
    turn = 2.0 * np.pi * np.outer(index + 0.25, index) / total
    twist = np.concatenate([np.cos(turn), np.sin(turn)], axis=1).astype(np.float32)
    return into, back, ahead, behind, twist


def halves(value):
    high = value.astype(BF)
    return high, (value - high.astype(F32)).astype(BF)


def dot(left, right):
    return jnp.dot(left, right, preferred_element_type=F32)


def coarse_stage(slabs, into, twist, high_ref, low_ref, row):
    high, low = halves(jnp.concatenate(slabs, axis=1))
    coarse = dot(into, jnp.concatenate([high, high, low], axis=0))
    cos, sin = twist[:, :SIDE], twist[:, SIDE:]
    for at in range(len(slabs)):
        real = coarse[:SIDE, at * SIDE : (at + 1) * SIDE]
        imag = coarse[SIDE:, at * SIDE : (at + 1) * SIDE]
        store_halves(
            jnp.concatenate([real * cos + imag * sin, imag * cos - real * sin], axis=1),
            high_ref, low_ref, row + at * SIDE,
        )


def store_halves(value, high_ref, low_ref, row):
    high, low = halves(value)
    rows = slice(row, row + value.shape[0])
    high_ref[rows, :] = high
    low_ref[rows, :] = low


def fine_stage(high_ref, low_ref, row, count, matrix, pieces=2):
    size = count // pieces
    results = []
    for at in range(pieces):
        rows = slice(row + at * size, row + (at + 1) * size)
        high, low = high_ref[rows, :], low_ref[rows, :]
        results.append(dot(jnp.concatenate([high, low, high], axis=1), matrix))
    return results


def last_stage(fine, back, twist):
    cos, sin = twist[:, :SIDE], twist[:, SIDE:]
    split = []
    for at in range(0, len(fine), 2):
        reals, imags = [], []
        for slab in fine[at : at + 2]:
            real, imag = slab[:, :SIDE], slab[:, SIDE:]
            reals.append(real * cos - imag * sin)
            imags.append(imag * cos + real * sin)
        turned = jnp.concatenate(
            [jnp.concatenate(reals, axis=1), jnp.concatenate(imags, axis=1)], axis=0
        )
        split.append(halves(turned))
    both = [dot(back, high) for high, _ in split]
    rest = [dot(back[:SIDE], low) for _, low in split]
    return [b[:SIDE] + b[SIDE:] + r for b, r in zip(both, rest)]


def slabs_of(parts):
    return [part[at : at + SIDE] for part in parts for at in range(0, part.shape[0], SIDE)]


def product(left, right):
    lr, li = left[:, :SIDE], left[:, SIDE:]
    rr, ri = right[:, :SIDE], right[:, SIDE:]
    return jnp.concatenate([lr * rr - li * ri, lr * ri + li * rr], axis=1)


def turned_product(left, right):
    lr, li = left[:, :SIDE], left[:, SIDE:]
    rr, ri = right[:, :SIDE], right[:, SIDE:]
    return jnp.concatenate([lr * rr + li * ri, lr * ri - li * rr], axis=1)


def gather_rows(ref, base, step, shards, pitch):
    return jnp.concatenate(
        [ref[pl.ds(base + q * step, shards, stride=pitch), :] for q in range(QUARTERS)], axis=0
    )


def pack_kernel(
    members, near_ref, k_hbm, v_hbm, g_hbm, q_hbm, f_hbm, out_ref,
    k_ref, v_ref, g_ref, q_ref, f_ref, sems,
):
    copies = []
    for q in range(QUARTERS):
        rows = pl.ds(q * SIDE, SIDE)
        pairs = ((k_hbm, k_ref), (v_hbm, v_ref), (g_hbm, g_ref), (q_hbm, q_ref))
        for at, (source, target) in enumerate(pairs):
            copy = pltpu.make_async_copy(source.at[rows], target.at[rows], sems.at[q * 4 + at])
            copy.start()
            copies.append(copy)
        if q == 0:
            start = pl.multiple_of(near_ref[0] * SIDE, SIDE)
            own = pltpu.make_async_copy(f_hbm.at[pl.ds(start, SIDE)], f_ref, sems.at[16])
            own.start()
    for q in range(QUARTERS):
        rows = slice(q * SIDE, (q + 1) * SIDE)
        for array, (left, right) in enumerate(((k_ref, v_ref), (g_ref, q_ref))):
            copies[q * 4 + array * 2].wait()
            copies[q * 4 + array * 2 + 1].wait()
            for h in range(HALVES):
                cols = slice(h * SIDE, (h + 1) * SIDE)
                at = array * 8 + h * QUARTERS + q
                out_ref[pl.ds(at, members, stride=IN_ROWS), :] = (
                    left[rows, cols] * right[rows, cols]
                ).T
        if q == 0:
            own.wait()
            out_ref[pl.ds(16, members, stride=IN_ROWS), :] = f_ref[...].T


def ahead_kernel(
    shards, in_ref, into_ref, back_ref, ahead_ref, behind_ref, twist_ref,
    corr_ref, gated_ref, grad_ref, high_ref, low_ref,
):
    into, twist = into_ref[...], twist_ref[...]
    pitch = shards * IN_ROWS
    span = BLOCKS * HALVES * SIDE
    half = span // 2
    total = None
    for part in range(2):
        for array in range(2):
            slabs = [
                gather_rows(
                    in_ref, block * pitch + array * 8 + h * QUARTERS, 1, shards, IN_ROWS
                )
                for block in (part * 2, part * 2 + 1)
                for h in range(HALVES)
            ]
            coarse_stage(slabs, into, twist, high_ref, low_ref, part * span + array * half)
    for part in range(2):
        both = fine_stage(high_ref, low_ref, part * span, span, ahead_ref[...], 1)[0]
        both = (both[:half], both[half:])
        rows = slice(part * half, (part + 1) * half)
        gated_ref[rows, :] = both[0]
        grad_ref[rows, :] = both[1]
        for at in range(0, half, SIDE):
            term = turned_product(both[0][at : at + SIDE], both[1][at : at + SIDE])
            total = term if total is None else total + term
    store_halves(total, high_ref, low_ref, 2 * span)
    fine = fine_stage(high_ref, low_ref, 2 * span, SIDE, behind_ref[...], 1)
    corr_ref[...] = last_stage([jnp.concatenate(fine, axis=0)], back_ref[...], twist)[0]


def behind_kernel(
    shards, in_ref, gated_ref, grad_ref, into_ref, back_ref, ahead_ref, behind_ref, twist_ref,
    out_ref, high_ref, low_ref,
):
    twist, back = twist_ref[...], back_ref[...]
    pitch = shards * OUT_ROWS
    group = 2 * HALVES * SIDE
    spare = BLOCKS * group
    slab = gather_rows(in_ref, 16, shards * IN_ROWS, shards, IN_ROWS)
    coarse_stage([slab], into_ref[...], twist, high_ref, low_ref, spare)
    filt = jnp.concatenate(fine_stage(high_ref, low_ref, spare, SIDE, ahead_ref[...]), axis=0)
    for block in range(BLOCKS):
        for array, spec_ref in enumerate((gated_ref, grad_ref)):
            combine = turned_product if array else product
            for h in range(HALVES):
                spec = spec_ref[pl.ds((block * 2 + h) * SIDE, SIDE), :]
                row = block * group + (array * HALVES + h) * SIDE
                store_halves(combine(filt, spec), high_ref, low_ref, row)
    for part in range(2):
        fine = slabs_of(
            fine_stage(high_ref, low_ref, part * 2 * group, 2 * group, behind_ref[...])
        )
        for near in range(2):
            block = part * 2 + near
            results = last_stage(fine[near * 4 : near * 4 + 4], back, twist)
            for at in range(2 * HALVES):
                column = at % 2 * SIDE
                for q in range(QUARTERS):
                    row = block * pitch + at * QUARTERS + q
                    out_ref[pl.ds(row, shards, stride=OUT_ROWS), :] = results[at // 2][
                        q * shards : (q + 1) * shards, column : column + SIDE
                    ]


def sum_kernel(shards, own_ref, other_ref, _, out_ref):
    total = own_ref[...] + other_ref[...]
    for block in range(BLOCKS):
        for q in range(QUARTERS):
            at = block * shards * OUT_ROWS + 16 + q
            out_ref[pl.ds(at, shards, stride=OUT_ROWS), :] = total[
                q * shards : (q + 1) * shards
            ]


def unpack_kernel(
    members, in_ref, g_ref, v_ref, k_ref, gq_hbm, gk_hbm, gv_hbm, gf_hbm,
    gq_ref, gk_ref, gv_ref, gf_ref, sems,
):
    copies = []
    for q in range(QUARTERS):
        rows = slice(q * SIDE, (q + 1) * SIDE)
        for h in range(HALVES):
            cols = slice(h * SIDE, (h + 1) * SIDE)
            at = h * QUARTERS + q
            conv = in_ref[pl.ds(at, members, stride=OUT_ROWS), :].T
            gq_ref[rows, cols] = conv * g_ref[rows, cols]
            back = in_ref[pl.ds(8 + at, members, stride=OUT_ROWS), :].T
            gk_ref[rows, cols] = back * v_ref[rows, cols]
            gv_ref[rows, cols] = back * k_ref[rows, cols]
        gf_ref[rows, :] = in_ref[pl.ds(16 + q, members, stride=OUT_ROWS), :].T
        pairs = ((gq_ref, gq_hbm), (gk_ref, gk_hbm), (gv_ref, gv_hbm), (gf_ref, gf_hbm))
        for at, (source, target) in enumerate(pairs):
            part = pl.ds(q * SIDE, SIDE)
            copy = pltpu.make_async_copy(source.at[part], target.at[part], sems.at[q * 4 + at])
            copy.start()
            copies.append(copy)
    for copy in copies:
        copy.wait()


VMEM = pl.BlockSpec(memory_space=pltpu.VMEM)
HBM = pl.BlockSpec(memory_space=pltpu.HBM)
SMEM = pl.BlockSpec(memory_space=pltpu.SMEM)
LIMIT = 24 * 1024 * 1024


def call(kernel, outs, args, name, ins=None, out_spec=VMEM, scratch=(), flops=0, aliases=None):
    moved = sum(4 * int(np.prod(shape)) for shape in outs)
    moved += sum(a.size * a.dtype.itemsize for a in args)
    return pl.pallas_call(
        kernel,
        out_shape=[jax.ShapeDtypeStruct(shape, F32) for shape in outs],
        in_specs=ins or [VMEM] * len(args),
        out_specs=[out_spec] * len(outs),
        scratch_shapes=list(scratch),
        input_output_aliases=aliases or {},
        name=name,
        compiler_params=pltpu.CompilerParams(vmem_limit_bytes=LIMIT),
        cost_estimate=pl.CostEstimate(flops=flops, bytes_accessed=moved, transcendentals=0),
    )(*args)


def exchange(block, inner):
    parted = block.reshape(block.shape[0] // int(np.prod(inner)), *inner, SIDE)
    return lax.all_to_all(parted, ("near", "seq"), 0, 0, tiled=True).reshape(block.shape)


def local(q_gate, k_gate, values, filter_raw, grad_out):
    shards = lax.axis_size("seq")
    members = shards * lax.axis_size("near")
    total = SIDE * SIDE
    into, back, ahead, behind, twist = (
        jnp.asarray(t) for t in tables(shards, total ** (-0.5) / total)
    )
    block = q_gate.shape
    wide = pltpu.VMEM(block, F32)
    split = [pltpu.VMEM((17 * SIDE, 2 * SIDE), BF)] * 2
    near = lax.axis_index("near").astype(jnp.int32).reshape(1)
    packed = call(
        functools.partial(pack_kernel, members),
        [(IN_ROWS * members, SIDE)],
        (near, *(pltpu.with_memory_space_constraint(a, pltpu.HBM) for a in (k_gate, values, grad_out, q_gate, filter_raw))),
        "pack",
        ins=[SMEM] + [HBM] * 5,
        scratch=[wide] * 4 + [pltpu.VMEM((SIDE, SIDE), F32), pltpu.SemaphoreType.DMA((17,))],
    )[0]
    spread = exchange(packed, (17, 1))
    corr, gated_spec, grad_spec = call(
        functools.partial(ahead_kernel, shards),
        [(SIDE, SIDE), (8 * SIDE, 2 * SIDE), (8 * SIDE, 2 * SIDE)],
        (spread, into, back, ahead, behind, twist),
        "ahead",
        scratch=split,
        flops=10**9,
    )
    other = lax.ppermute(corr, "far", [(0, 1), (1, 0)])
    results = call(
        functools.partial(behind_kernel, shards),
        [(OUT_ROWS * members, SIDE)],
        (spread, gated_spec, grad_spec, into, back, ahead, behind, twist),
        "behind",
        scratch=split,
        flops=10**9,
    )[0]
    results = call(
        functools.partial(sum_kernel, shards),
        [(OUT_ROWS * members, SIDE)],
        (corr, other, results),
        "sum",
        ins=[VMEM] * 3,
        aliases={2: 0},
    )[0]
    placed = exchange(results, (5, 4))
    grad_q, grad_k, grad_v, grad_filter = call(
        functools.partial(unpack_kernel, members),
        [block, block, block, filter_raw.shape],
        (placed, grad_out, values, k_gate),
        "unpack",
        out_spec=HBM,
        scratch=[wide] * 3 + [pltpu.VMEM(filter_raw.shape, F32), pltpu.SemaphoreType.DMA((16,))],
    )
    return grad_q, grad_k, grad_v, grad_filter


def solution(mesh):
    shards, groups = mesh.devices.shape
    parted = Mesh(
        mesh.devices.reshape(shards, groups // BLOCKS, BLOCKS), ("seq", "far", "near")
    )
    whole, filters = P("seq", ("far", "near")), P("seq", None)
    return jax.shard_map(
        local,
        mesh=parted,
        in_specs=(whole, whole, whole, filters, whole),
        out_specs=(whole, whole, whole, filters),
        check_vma=False,
    )
```

```python
import functools

import jax
import jax.numpy as jnp
import numpy as np
from jax import lax
from jax.experimental import pallas as pl
from jax.experimental.pallas import tpu as pltpu
from jax.sharding import Mesh
from jax.sharding import PartitionSpec as P


SIDE = 128
HALVES = 2
BLOCKS = 4
QUARTERS = 4
IN_ROWS = 17
OUT_ROWS = 20
BF = jnp.bfloat16
F32 = jnp.float32


def split_np(table):
    high = table.astype(np.float32).astype(BF)
    low = (table - high.astype(np.float64)).astype(np.float32).astype(BF)
    return high, low


def tables(shards, factor):
    total = SIDE * SIDE
    index = np.arange(SIDE)
    quarter, source = np.divmod(index, shards)
    first = source * QUARTERS + quarter
    coarse = 2.0 * np.pi * np.outer(index + 0.25, first) / SIDE
    high, low = split_np(np.concatenate([np.cos(coarse), -np.sin(coarse)], axis=0))
    into = np.concatenate([high, low, high], axis=1)
    high, low = split_np(np.concatenate([np.cos(coarse.T), -np.sin(coarse.T)], axis=1) * factor)
    back = np.concatenate([high, low], axis=0)
    fine = 2.0 * np.pi * (np.outer(index, index) % SIDE) / SIDE
    cos, sin = np.cos(fine), np.sin(fine)
    high, low = split_np(np.block([[cos, -sin], [sin, cos]]))
    ahead = np.concatenate([high, high, low], axis=0)
    high, low = split_np(np.block([[cos, sin], [-sin, cos]]))
    behind = np.concatenate([high, high, low], axis=0)
    turn = 2.0 * np.pi * np.outer(index + 0.25, index) / total
    twist = np.concatenate([np.cos(turn), np.sin(turn)], axis=1).astype(np.float32)
    return into, back, ahead, behind, twist


def halves(value):
    high = value.astype(BF)
    return high, (value - high.astype(F32)).astype(BF)


def dot(left, right):
    return jnp.dot(left, right, preferred_element_type=F32)


def coarse_stage(slabs, into, twist, high_ref, low_ref, row):
    high, low = halves(jnp.concatenate(slabs, axis=1))
    coarse = dot(into, jnp.concatenate([high, high, low], axis=0))
    cos, sin = twist[:, :SIDE], twist[:, SIDE:]
    for at in range(len(slabs)):
        real = coarse[:SIDE, at * SIDE : (at + 1) * SIDE]
        imag = coarse[SIDE:, at * SIDE : (at + 1) * SIDE]
        store_halves(
            jnp.concatenate([real * cos + imag * sin, imag * cos - real * sin], axis=1),
            high_ref, low_ref, row + at * SIDE,
        )


def store_halves(value, high_ref, low_ref, row):
    high, low = halves(value)
    rows = slice(row, row + value.shape[0])
    high_ref[rows, :] = high
    low_ref[rows, :] = low


def fine_stage(high_ref, low_ref, row, count, matrix, pieces=2):
    size = count // pieces
    results = []
    for at in range(pieces):
        rows = slice(row + at * size, row + (at + 1) * size)
        high, low = high_ref[rows, :], low_ref[rows, :]
        results.append(dot(jnp.concatenate([high, low, high], axis=1), matrix))
    return results


def last_stage(fine, back, twist):
    cos, sin = twist[:, :SIDE], twist[:, SIDE:]
    split = []
    for at in range(0, len(fine), 2):
        reals, imags = [], []
        for slab in fine[at : at + 2]:
            real, imag = slab[:, :SIDE], slab[:, SIDE:]
            reals.append(real * cos - imag * sin)
            imags.append(imag * cos + real * sin)
        turned = jnp.concatenate(
            [jnp.concatenate(reals, axis=1), jnp.concatenate(imags, axis=1)], axis=0
        )
        split.append(halves(turned))
    both = [dot(back, high) for high, _ in split]
    rest = [dot(back[:SIDE], low) for _, low in split]
    return [b[:SIDE] + b[SIDE:] + r for b, r in zip(both, rest)]


def slabs_of(parts):
    return [part[at : at + SIDE] for part in parts for at in range(0, part.shape[0], SIDE)]


def product(left, right):
    lr, li = left[:, :SIDE], left[:, SIDE:]
    rr, ri = right[:, :SIDE], right[:, SIDE:]
    return jnp.concatenate([lr * rr - li * ri, lr * ri + li * rr], axis=1)


def turned_product(left, right):
    lr, li = left[:, :SIDE], left[:, SIDE:]
    rr, ri = right[:, :SIDE], right[:, SIDE:]
    return jnp.concatenate([lr * rr + li * ri, lr * ri - li * rr], axis=1)


def gather_rows(ref, base, step, shards, pitch):
    return jnp.concatenate(
        [ref[pl.ds(base + q * step, shards, stride=pitch), :] for q in range(QUARTERS)], axis=0
    )


def pack_kernel(
    members, place_ref, k_hbm, v_hbm, g_hbm, q_hbm, f_hbm, own_ref, other_ref,
    k_ref, v_ref, g_ref, q_ref, f_ref, sems,
):
    copies = []
    for q in range(QUARTERS):
        rows = pl.ds(q * SIDE, SIDE)
        pairs = ((k_hbm, k_ref), (v_hbm, v_ref), (g_hbm, g_ref), (q_hbm, q_ref))
        for at, (source, target) in enumerate(pairs):
            copy = pltpu.make_async_copy(source.at[rows], target.at[rows], sems.at[q * 4 + at])
            copy.start()
            copies.append(copy)
        if q == 0:
            start = pl.multiple_of(place_ref[0] * SIDE, SIDE)
            part = pltpu.make_async_copy(f_hbm.at[pl.ds(start, SIDE)], f_ref, sems.at[16])
            part.start()
    core = place_ref[1]
    first = core == 0

    def put(slab, at):
        lower, upper = slab[:members], slab[members:]
        own_ref[pl.ds(core * IN_ROWS + at, members, stride=2 * IN_ROWS), :] = jnp.where(
            first, lower, upper
        )
        other_ref[pl.ds(at, members, stride=IN_ROWS), :] = jnp.where(first, upper, lower)

    for q in range(QUARTERS):
        rows = slice(q * SIDE, (q + 1) * SIDE)
        for array, (left, right) in enumerate(((k_ref, v_ref), (g_ref, q_ref))):
            copies[q * 4 + array * 2].wait()
            copies[q * 4 + array * 2 + 1].wait()
            for h in range(HALVES):
                cols = slice(h * SIDE, (h + 1) * SIDE)
                put((left[rows, cols] * right[rows, cols]).T, array * 8 + h * QUARTERS + q)
        if q == 0:
            part.wait()
            put(f_ref[...].T, 16)


def merge_kernel(members, place_ref, other_ref, _, out_ref):
    start = (1 - place_ref[1]) * IN_ROWS
    for at in range(IN_ROWS):
        out_ref[pl.ds(start + at, members, stride=2 * IN_ROWS), :] = other_ref[
            pl.ds(at, members, stride=IN_ROWS), :
        ]


def ahead_kernel(
    shards, in_ref, into_ref, back_ref, ahead_ref, behind_ref, twist_ref,
    corr_ref, gated_ref, grad_ref, high_ref, low_ref,
):
    into, twist = into_ref[...], twist_ref[...]
    pitch = shards * IN_ROWS
    span = BLOCKS * HALVES * SIDE
    half = span // 2
    total = None
    for part in range(2):
        for array in range(2):
            slabs = [
                gather_rows(
                    in_ref, block * pitch + array * 8 + h * QUARTERS, 1, shards, IN_ROWS
                )
                for block in (part * 2, part * 2 + 1)
                for h in range(HALVES)
            ]
            coarse_stage(slabs, into, twist, high_ref, low_ref, part * span + array * half)
    for part in range(2):
        both = fine_stage(high_ref, low_ref, part * span, span, ahead_ref[...], 1)[0]
        both = (both[:half], both[half:])
        rows = slice(part * half, (part + 1) * half)
        gated_ref[rows, :] = both[0]
        grad_ref[rows, :] = both[1]
        for at in range(0, half, SIDE):
            term = turned_product(both[0][at : at + SIDE], both[1][at : at + SIDE])
            total = term if total is None else total + term
    store_halves(total, high_ref, low_ref, 2 * span)
    fine = fine_stage(high_ref, low_ref, 2 * span, SIDE, behind_ref[...], 1)
    corr_ref[...] = last_stage([jnp.concatenate(fine, axis=0)], back_ref[...], twist)[0]


def behind_kernel(
    shards, in_ref, gated_ref, grad_ref, into_ref, back_ref, ahead_ref, behind_ref, twist_ref,
    out_ref, high_ref, low_ref,
):
    twist, back = twist_ref[...], back_ref[...]
    pitch = shards * OUT_ROWS
    group = 2 * HALVES * SIDE
    spare = BLOCKS * group
    slab = gather_rows(in_ref, 16, shards * IN_ROWS, shards, IN_ROWS)
    coarse_stage([slab], into_ref[...], twist, high_ref, low_ref, spare)
    filt = jnp.concatenate(fine_stage(high_ref, low_ref, spare, SIDE, ahead_ref[...]), axis=0)
    for block in range(BLOCKS):
        for array, spec_ref in enumerate((gated_ref, grad_ref)):
            combine = turned_product if array else product
            for h in range(HALVES):
                spec = spec_ref[pl.ds((block * 2 + h) * SIDE, SIDE), :]
                row = block * group + (array * HALVES + h) * SIDE
                store_halves(combine(filt, spec), high_ref, low_ref, row)
    for part in range(2):
        fine = slabs_of(
            fine_stage(high_ref, low_ref, part * 2 * group, 2 * group, behind_ref[...])
        )
        for near in range(2):
            block = part * 2 + near
            results = last_stage(fine[near * 4 : near * 4 + 4], back, twist)
            for at in range(2 * HALVES):
                column = at % 2 * SIDE
                for q in range(QUARTERS):
                    row = block * pitch + at * QUARTERS + q
                    out_ref[pl.ds(row, shards, stride=OUT_ROWS), :] = results[at // 2][
                        q * shards : (q + 1) * shards, column : column + SIDE
                    ]


def sum_kernel(shards, own_ref, other_ref, _, out_ref):
    total = own_ref[...] + other_ref[...]
    for block in range(BLOCKS):
        for q in range(QUARTERS):
            at = block * shards * OUT_ROWS + 16 + q
            out_ref[pl.ds(at, shards, stride=OUT_ROWS), :] = total[
                q * shards : (q + 1) * shards
            ]


def unpack_kernel(
    members, in_ref, g_ref, v_ref, k_ref, gq_hbm, gk_hbm, gv_hbm, gf_hbm,
    gq_ref, gk_ref, gv_ref, gf_ref, sems,
):
    def get(at):
        parts = [
            in_ref[pl.ds(core * OUT_ROWS + at, members, stride=2 * OUT_ROWS), :]
            for core in range(2)
        ]
        return jnp.concatenate(parts, axis=0).T

    copies = []
    for q in range(QUARTERS):
        rows = slice(q * SIDE, (q + 1) * SIDE)
        for h in range(HALVES):
            cols = slice(h * SIDE, (h + 1) * SIDE)
            at = h * QUARTERS + q
            gq_ref[rows, cols] = get(at) * g_ref[rows, cols]
            back = get(8 + at)
            gk_ref[rows, cols] = back * v_ref[rows, cols]
            gv_ref[rows, cols] = back * k_ref[rows, cols]
        gf_ref[rows, :] = get(16 + q)
        pairs = ((gq_ref, gq_hbm), (gk_ref, gk_hbm), (gv_ref, gv_hbm), (gf_ref, gf_hbm))
        for at, (source, target) in enumerate(pairs):
            part = pl.ds(q * SIDE, SIDE)
            copy = pltpu.make_async_copy(source.at[part], target.at[part], sems.at[q * 4 + at])
            copy.start()
            copies.append(copy)
    for copy in copies:
        copy.wait()


VMEM = pl.BlockSpec(memory_space=pltpu.VMEM)
HBM = pl.BlockSpec(memory_space=pltpu.HBM)
SMEM = pl.BlockSpec(memory_space=pltpu.SMEM)
LIMIT = 24 * 1024 * 1024


def call(kernel, outs, args, name, ins=None, out_spec=VMEM, scratch=(), flops=0, aliases=None):
    moved = sum(4 * int(np.prod(shape)) for shape in outs)
    moved += sum(a.size * a.dtype.itemsize for a in args)
    return pl.pallas_call(
        kernel,
        out_shape=[jax.ShapeDtypeStruct(shape, F32) for shape in outs],
        in_specs=ins or [VMEM] * len(args),
        out_specs=[out_spec] * len(outs),
        scratch_shapes=list(scratch),
        input_output_aliases=aliases or {},
        name=name,
        compiler_params=pltpu.CompilerParams(vmem_limit_bytes=LIMIT),
        cost_estimate=pl.CostEstimate(flops=flops, bytes_accessed=moved, transcendentals=0),
    )(*args)


def exchange(block, inner, axes):
    parted = block.reshape(block.shape[0] // int(np.prod(inner)), *inner, SIDE)
    return lax.all_to_all(parted, axes, 0, 0, tiled=True).reshape(block.shape)


def local(q_gate, k_gate, values, filter_raw, grad_out):
    members = lax.axis_size("line") * lax.axis_size("near")
    shards = lax.axis_size("line") * lax.axis_size("core")
    total = SIDE * SIDE
    into, back, ahead, behind, twist = (
        jnp.asarray(t) for t in tables(shards, total ** (-0.5) / total)
    )
    block = q_gate.shape
    wide = pltpu.VMEM(block, F32)
    split = [pltpu.VMEM((17 * SIDE, 2 * SIDE), BF)] * 2
    place = jnp.stack([lax.axis_index("near"), lax.axis_index("core")]).astype(jnp.int32)
    swap = [(0, 1), (1, 0)]
    inputs = (k_gate, values, grad_out, q_gate, filter_raw)
    packed, other = call(
        functools.partial(pack_kernel, members),
        [(2 * IN_ROWS * members, SIDE), (IN_ROWS * members, SIDE)],
        (place, *(pltpu.with_memory_space_constraint(a, pltpu.HBM) for a in inputs)),
        "pack",
        ins=[SMEM] + [HBM] * 5,
        scratch=[wide] * 4 + [pltpu.VMEM((SIDE, SIDE), F32), pltpu.SemaphoreType.DMA((17,))],
    )
    packed = call(
        functools.partial(merge_kernel, members),
        [(2 * IN_ROWS * members, SIDE)],
        (place, lax.ppermute(other, "core", swap), packed),
        "merge",
        ins=[SMEM, VMEM, VMEM],
        aliases={2: 0},
    )[0]
    spread = exchange(packed, (17, 2), ("near", "line"))
    corr, gated_spec, grad_spec = call(
        functools.partial(ahead_kernel, shards),
        [(SIDE, SIDE), (8 * SIDE, 2 * SIDE), (8 * SIDE, 2 * SIDE)],
        (spread, into, back, ahead, behind, twist),
        "ahead",
        scratch=split,
        flops=10**9,
    )
    other = lax.ppermute(corr, "far", swap)
    results = call(
        functools.partial(behind_kernel, shards),
        [(2 * OUT_ROWS * members, SIDE)],
        (spread, gated_spec, grad_spec, into, back, ahead, behind, twist),
        "behind",
        scratch=split,
        flops=10**9,
    )[0]
    results = call(
        functools.partial(sum_kernel, shards),
        [(2 * OUT_ROWS * members, SIDE)],
        (corr, other, results),
        "sum",
        ins=[VMEM] * 3,
        aliases={2: 0},
    )[0]
    placed = exchange(results, (5, 4), ("near", "line", "core"))
    grad_q, grad_k, grad_v, grad_filter = call(
        functools.partial(unpack_kernel, members),
        [block, block, block, filter_raw.shape],
        (placed, grad_out, values, k_gate),
        "unpack",
        out_spec=HBM,
        scratch=[wide] * 3 + [pltpu.VMEM(filter_raw.shape, F32), pltpu.SemaphoreType.DMA((16,))],
    )
    return grad_q, grad_k, grad_v, grad_filter


def solution(mesh):
    shards, groups = mesh.devices.shape
    parted = Mesh(
        mesh.devices.reshape(shards // 2, 2, groups // BLOCKS, BLOCKS),
        ("line", "core", "far", "near"),
    )
    whole, filters = P(("line", "core"), ("far", "near")), P(("line", "core"), None)
    return jax.shard_map(
        local,
        mesh=parted,
        in_specs=(whole, whole, whole, filters, whole),
        out_specs=(whole, whole, whole, filters),
        check_vma=False,
    )
```

```python
import functools

import jax
import jax.numpy as jnp
import numpy as np
from jax import lax
from jax.experimental import pallas as pl
from jax.experimental.pallas import tpu as pltpu
from jax.sharding import Mesh
from jax.sharding import PartitionSpec as P


SIDE = 128
HALVES = 2
BLOCKS = 4
QUARTERS = 4
IN_ROWS = 17
OUT_ROWS = 20
BF = jnp.bfloat16
F32 = jnp.float32


def split_np(table):
    high = table.astype(np.float32).astype(BF)
    low = (table - high.astype(np.float64)).astype(np.float32).astype(BF)
    return high, low


def tables(shards, factor):
    total = SIDE * SIDE
    index = np.arange(SIDE)
    quarter, source = np.divmod(index, shards)
    first = source * QUARTERS + quarter
    coarse = 2.0 * np.pi * np.outer(index + 0.25, first) / SIDE
    high, low = split_np(np.concatenate([np.cos(coarse), -np.sin(coarse)], axis=0))
    into = np.concatenate([high, low, high], axis=1)
    high, low = split_np(np.concatenate([np.cos(coarse.T), -np.sin(coarse.T)], axis=1) * factor)
    back = np.concatenate([high, low], axis=0)
    fine = 2.0 * np.pi * (np.outer(index, index) % SIDE) / SIDE
    cos, sin = np.cos(fine), np.sin(fine)
    high, low = split_np(np.block([[cos, -sin], [sin, cos]]))
    ahead = np.concatenate([high, high, low], axis=0)
    high, low = split_np(np.block([[cos, sin], [-sin, cos]]))
    behind = np.concatenate([high, high, low], axis=0)
    turn = 2.0 * np.pi * np.outer(index + 0.25, index) / total
    twist = np.concatenate([np.cos(turn), np.sin(turn)], axis=1).astype(np.float32)
    return into, back, ahead, behind, twist


def halves(value):
    high = value.astype(BF)
    return high, (value - high.astype(F32)).astype(BF)


def dot(left, right):
    return jnp.dot(left, right, preferred_element_type=F32)


def coarse_stage(slabs, into, twist, high_ref, low_ref, row):
    high, low = halves(jnp.concatenate(slabs, axis=1))
    coarse = dot(into, jnp.concatenate([high, high, low], axis=0))
    cos, sin = twist[:, :SIDE], twist[:, SIDE:]
    for at in range(len(slabs)):
        real = coarse[:SIDE, at * SIDE : (at + 1) * SIDE]
        imag = coarse[SIDE:, at * SIDE : (at + 1) * SIDE]
        store_halves(
            jnp.concatenate([real * cos + imag * sin, imag * cos - real * sin], axis=1),
            high_ref, low_ref, row + at * SIDE,
        )


def store_halves(value, high_ref, low_ref, row):
    high, low = halves(value)
    rows = slice(row, row + value.shape[0])
    high_ref[rows, :] = high
    low_ref[rows, :] = low


def fine_stage(high_ref, low_ref, row, count, matrix, pieces=2):
    size = count // pieces
    results = []
    for at in range(pieces):
        rows = slice(row + at * size, row + (at + 1) * size)
        high, low = high_ref[rows, :], low_ref[rows, :]
        results.append(dot(jnp.concatenate([high, low, high], axis=1), matrix))
    return results


def last_stage(fine, back, twist):
    cos, sin = twist[:, :SIDE], twist[:, SIDE:]
    split = []
    for at in range(0, len(fine), 2):
        reals, imags = [], []
        for slab in fine[at : at + 2]:
            real, imag = slab[:, :SIDE], slab[:, SIDE:]
            reals.append(real * cos - imag * sin)
            imags.append(imag * cos + real * sin)
        turned = jnp.concatenate(
            [jnp.concatenate(reals, axis=1), jnp.concatenate(imags, axis=1)], axis=0
        )
        split.append(halves(turned))
    both = [dot(back, high) for high, _ in split]
    rest = [dot(back[:SIDE], low) for _, low in split]
    return [b[:SIDE] + b[SIDE:] + r for b, r in zip(both, rest)]


def slabs_of(parts):
    return [part[at : at + SIDE] for part in parts for at in range(0, part.shape[0], SIDE)]


def product(left, right):
    lr, li = left[:, :SIDE], left[:, SIDE:]
    rr, ri = right[:, :SIDE], right[:, SIDE:]
    return jnp.concatenate([lr * rr - li * ri, lr * ri + li * rr], axis=1)


def turned_product(left, right):
    lr, li = left[:, :SIDE], left[:, SIDE:]
    rr, ri = right[:, :SIDE], right[:, SIDE:]
    return jnp.concatenate([lr * rr + li * ri, lr * ri - li * rr], axis=1)


def gather_rows(ref, base, step, shards, pitch):
    return jnp.concatenate(
        [ref[pl.ds(base + q * step, shards, stride=pitch), :] for q in range(QUARTERS)], axis=0
    )


def pack_kernel(
    members, near_ref, k_hbm, v_hbm, g_hbm, q_hbm, f_hbm, out_ref,
    k_ref, v_ref, g_ref, q_ref, f_ref, sems,
):
    copies = []
    for part in range(2):
        rows = pl.ds(part * 2 * SIDE, 2 * SIDE)
        pairs = ((k_hbm, k_ref), (v_hbm, v_ref), (g_hbm, g_ref), (q_hbm, q_ref))
        for at, (source, target) in enumerate(pairs):
            copy = pltpu.make_async_copy(source.at[rows], target.at[rows], sems.at[part * 4 + at])
            copy.start()
            copies.append(copy)
        if part == 0:
            start = pl.multiple_of(near_ref[0] * SIDE, SIDE)
            own = pltpu.make_async_copy(f_hbm.at[pl.ds(start, SIDE)], f_ref, sems.at[16])
            own.start()
    for part in range(2):
        for array, (left, right) in enumerate(((k_ref, v_ref), (g_ref, q_ref))):
            copies[part * 4 + array * 2].wait()
            copies[part * 4 + array * 2 + 1].wait()
            for q in (2 * part, 2 * part + 1):
                rows = slice(q * SIDE, (q + 1) * SIDE)
                for h in range(HALVES):
                    cols = slice(h * SIDE, (h + 1) * SIDE)
                    at = array * 8 + h * QUARTERS + q
                    out_ref[pl.ds(at, members, stride=IN_ROWS), :] = (
                        left[rows, cols] * right[rows, cols]
                    ).T
        if part == 0:
            own.wait()
            out_ref[pl.ds(16, members, stride=IN_ROWS), :] = f_ref[...].T


def ahead_kernel(
    shards, in_ref, into_ref, back_ref, ahead_ref, behind_ref, twist_ref,
    corr_ref, gated_ref, grad_ref, high_ref, low_ref,
):
    into, twist = into_ref[...], twist_ref[...]
    pitch = shards * IN_ROWS
    span = BLOCKS * HALVES * SIDE
    half = span // 2
    total = None
    for part in range(2):
        for array in range(2):
            slabs = [
                gather_rows(
                    in_ref, block * pitch + array * 8 + h * QUARTERS, 1, shards, IN_ROWS
                )
                for block in (part * 2, part * 2 + 1)
                for h in range(HALVES)
            ]
            coarse_stage(slabs, into, twist, high_ref, low_ref, part * span + array * half)
    for part in range(2):
        both = fine_stage(high_ref, low_ref, part * span, span, ahead_ref[...], 1)[0]
        both = (both[:half], both[half:])
        rows = slice(part * half, (part + 1) * half)
        gated_ref[rows, :] = both[0]
        grad_ref[rows, :] = both[1]
        for at in range(0, half, SIDE):
            term = turned_product(both[0][at : at + SIDE], both[1][at : at + SIDE])
            total = term if total is None else total + term
    store_halves(total, high_ref, low_ref, 2 * span)
    fine = fine_stage(high_ref, low_ref, 2 * span, SIDE, behind_ref[...], 1)
    corr_ref[...] = last_stage([jnp.concatenate(fine, axis=0)], back_ref[...], twist)[0]


def behind_kernel(
    shards, in_ref, gated_ref, grad_ref, into_ref, back_ref, ahead_ref, behind_ref, twist_ref,
    out_ref, high_ref, low_ref,
):
    twist, back = twist_ref[...], back_ref[...]
    pitch = shards * OUT_ROWS
    group = 2 * HALVES * SIDE
    spare = BLOCKS * group
    slab = gather_rows(in_ref, 16, shards * IN_ROWS, shards, IN_ROWS)
    coarse_stage([slab], into_ref[...], twist, high_ref, low_ref, spare)
    filt = jnp.concatenate(fine_stage(high_ref, low_ref, spare, SIDE, ahead_ref[...]), axis=0)
    for block in range(BLOCKS):
        for array, spec_ref in enumerate((gated_ref, grad_ref)):
            combine = turned_product if array else product
            for h in range(HALVES):
                spec = spec_ref[pl.ds((block * 2 + h) * SIDE, SIDE), :]
                row = block * group + (array * HALVES + h) * SIDE
                store_halves(combine(filt, spec), high_ref, low_ref, row)
    for part in range(2):
        fine = slabs_of(
            fine_stage(high_ref, low_ref, part * 2 * group, 2 * group, behind_ref[...])
        )
        for near in range(2):
            block = part * 2 + near
            results = last_stage(fine[near * 4 : near * 4 + 4], back, twist)
            for at in range(2 * HALVES):
                column = at % 2 * SIDE
                for q in range(QUARTERS):
                    row = block * pitch + at * QUARTERS + q
                    out_ref[pl.ds(row, shards, stride=OUT_ROWS), :] = results[at // 2][
                        q * shards : (q + 1) * shards, column : column + SIDE
                    ]


def sum_kernel(shards, own_ref, other_ref, _, out_ref):
    total = own_ref[...] + other_ref[...]
    for block in range(BLOCKS):
        for q in range(QUARTERS):
            at = block * shards * OUT_ROWS + 16 + q
            out_ref[pl.ds(at, shards, stride=OUT_ROWS), :] = total[
                q * shards : (q + 1) * shards
            ]


def unpack_kernel(
    members, in_ref, g_ref, v_ref, k_ref, gq_hbm, gk_hbm, gv_hbm, gf_hbm,
    gq_ref, gk_ref, gv_ref, gf_ref, sems,
):
    copies = []

    def send(source, target, q):
        part = pl.ds(q * SIDE, SIDE)
        copy = pltpu.make_async_copy(source.at[part], target.at[part], sems.at[len(copies)])
        copy.start()
        copies.append(copy)

    for q in range(QUARTERS):
        rows = slice(q * SIDE, (q + 1) * SIDE)
        for h in range(HALVES):
            cols = slice(h * SIDE, (h + 1) * SIDE)
            back = in_ref[pl.ds(8 + h * QUARTERS + q, members, stride=OUT_ROWS), :].T
            gk_ref[rows, cols] = back * v_ref[rows, cols]
            gv_ref[rows, cols] = back * k_ref[rows, cols]
        send(gk_ref, gk_hbm, q)
        send(gv_ref, gv_hbm, q)
        for h in range(HALVES):
            cols = slice(h * SIDE, (h + 1) * SIDE)
            conv = in_ref[pl.ds(h * QUARTERS + q, members, stride=OUT_ROWS), :].T
            gq_ref[rows, cols] = conv * g_ref[rows, cols]
        send(gq_ref, gq_hbm, q)
        gf_ref[rows, :] = in_ref[pl.ds(16 + q, members, stride=OUT_ROWS), :].T
        send(gf_ref, gf_hbm, q)
    for copy in copies:
        copy.wait()


VMEM = pl.BlockSpec(memory_space=pltpu.VMEM)
HBM = pl.BlockSpec(memory_space=pltpu.HBM)
SMEM = pl.BlockSpec(memory_space=pltpu.SMEM)
LIMIT = 24 * 1024 * 1024


def call(kernel, outs, args, name, ins=None, out_spec=VMEM, scratch=(), flops=0, aliases=None):
    moved = sum(4 * int(np.prod(shape)) for shape in outs)
    moved += sum(a.size * a.dtype.itemsize for a in args)
    return pl.pallas_call(
        kernel,
        out_shape=[jax.ShapeDtypeStruct(shape, F32) for shape in outs],
        in_specs=ins or [VMEM] * len(args),
        out_specs=[out_spec] * len(outs),
        scratch_shapes=list(scratch),
        input_output_aliases=aliases or {},
        name=name,
        compiler_params=pltpu.CompilerParams(vmem_limit_bytes=LIMIT),
        cost_estimate=pl.CostEstimate(flops=flops, bytes_accessed=moved, transcendentals=0),
    )(*args)


def exchange(block, inner):
    parted = block.reshape(block.shape[0] // int(np.prod(inner)), *inner, SIDE)
    return lax.all_to_all(parted, ("near", "seq"), 0, 0, tiled=True).reshape(block.shape)


def local(q_gate, k_gate, values, filter_raw, grad_out):
    shards = lax.axis_size("seq")
    members = shards * lax.axis_size("near")
    total = SIDE * SIDE
    into, back, ahead, behind, twist = (
        jnp.asarray(t) for t in tables(shards, total ** (-0.5) / total)
    )
    block = q_gate.shape
    wide = pltpu.VMEM(block, F32)
    split = [pltpu.VMEM((17 * SIDE, 2 * SIDE), BF)] * 2
    near = lax.axis_index("near").astype(jnp.int32).reshape(1)
    packed = call(
        functools.partial(pack_kernel, members),
        [(IN_ROWS * members, SIDE)],
        (near, *(pltpu.with_memory_space_constraint(a, pltpu.HBM) for a in (k_gate, values, grad_out, q_gate, filter_raw))),
        "pack",
        ins=[SMEM] + [HBM] * 5,
        scratch=[wide] * 4 + [pltpu.VMEM((SIDE, SIDE), F32), pltpu.SemaphoreType.DMA((17,))],
    )[0]
    spread = exchange(packed, (17, 1))
    corr, gated_spec, grad_spec = call(
        functools.partial(ahead_kernel, shards),
        [(SIDE, SIDE), (8 * SIDE, 2 * SIDE), (8 * SIDE, 2 * SIDE)],
        (spread, into, back, ahead, behind, twist),
        "ahead",
        scratch=split,
        flops=10**9,
    )
    other = lax.ppermute(corr, "far", [(0, 1), (1, 0)])
    results = call(
        functools.partial(behind_kernel, shards),
        [(OUT_ROWS * members, SIDE)],
        (spread, gated_spec, grad_spec, into, back, ahead, behind, twist),
        "behind",
        scratch=split,
        flops=10**9,
    )[0]
    results = call(
        functools.partial(sum_kernel, shards),
        [(OUT_ROWS * members, SIDE)],
        (corr, other, results),
        "sum",
        ins=[VMEM] * 3,
        aliases={2: 0},
    )[0]
    placed = exchange(results, (5, 4))
    grad_q, grad_k, grad_v, grad_filter = call(
        functools.partial(unpack_kernel, members),
        [block, block, block, filter_raw.shape],
        (placed, grad_out, values, k_gate),
        "unpack",
        out_spec=HBM,
        scratch=[wide] * 3 + [pltpu.VMEM(filter_raw.shape, F32), pltpu.SemaphoreType.DMA((16,))],
    )
    return grad_q, grad_k, grad_v, grad_filter


def solution(mesh):
    shards, groups = mesh.devices.shape
    parted = Mesh(
        mesh.devices.reshape(shards, groups // BLOCKS, BLOCKS), ("seq", "far", "near")
    )
    whole, filters = P("seq", ("far", "near")), P("seq", None)
    return jax.shard_map(
        local,
        mesh=parted,
        in_specs=(whole, whole, whole, filters, whole),
        out_specs=(whole, whole, whole, filters),
        check_vma=False,
    )
```

```python
import functools

import jax
import jax.numpy as jnp
import numpy as np
from jax import lax
from jax.experimental import pallas as pl
from jax.experimental.pallas import tpu as pltpu
from jax.sharding import Mesh
from jax.sharding import PartitionSpec as P


SIDE = 128
HALVES = 2
BLOCKS = 4
QUARTERS = 4
IN_ROWS = 17
OUT_ROWS = 20
BF = jnp.bfloat16
F32 = jnp.float32


def split_np(table):
    high = table.astype(np.float32).astype(BF)
    low = (table - high.astype(np.float64)).astype(np.float32).astype(BF)
    return high, low


def tables(shards, factor):
    total = SIDE * SIDE
    index = np.arange(SIDE)
    quarter, source = np.divmod(index, shards)
    first = source * QUARTERS + quarter
    coarse = 2.0 * np.pi * np.outer(index + 0.25, first) / SIDE
    high, low = split_np(np.concatenate([np.cos(coarse), -np.sin(coarse)], axis=0))
    into = np.concatenate([high, low, high], axis=1)
    high, low = split_np(np.concatenate([np.cos(coarse.T), -np.sin(coarse.T)], axis=1) * factor)
    back = np.concatenate([high, low], axis=0)
    fine = 2.0 * np.pi * (np.outer(index, index) % SIDE) / SIDE
    cos, sin = np.cos(fine), np.sin(fine)
    high, low = split_np(np.block([[cos, -sin], [sin, cos]]))
    ahead = np.concatenate([high, high, low], axis=0)
    high, low = split_np(np.block([[cos, sin], [-sin, cos]]))
    behind = np.concatenate([high, high, low], axis=0)
    turn = 2.0 * np.pi * np.outer(index + 0.25, index) / total
    twist = np.concatenate([np.cos(turn), np.sin(turn)], axis=1).astype(np.float32)
    return into, back, ahead, behind, twist


def halves(value):
    high = value.astype(BF)
    return high, (value - high.astype(F32)).astype(BF)


def dot(left, right):
    return jnp.dot(left, right, preferred_element_type=F32)


def coarse_stage(slabs, into, twist, high_ref, low_ref, row):
    high, low = halves(jnp.concatenate(slabs, axis=1))
    coarse = dot(into, jnp.concatenate([high, high, low], axis=0))
    cos, sin = twist[:, :SIDE], twist[:, SIDE:]
    for at in range(len(slabs)):
        real = coarse[:SIDE, at * SIDE : (at + 1) * SIDE]
        imag = coarse[SIDE:, at * SIDE : (at + 1) * SIDE]
        store_halves(
            jnp.concatenate([real * cos + imag * sin, imag * cos - real * sin], axis=1),
            high_ref, low_ref, row + at * SIDE,
        )


def store_halves(value, high_ref, low_ref, row):
    high, low = halves(value)
    rows = slice(row, row + value.shape[0])
    high_ref[rows, :] = high
    low_ref[rows, :] = low


def fine_stage(high_ref, low_ref, row, count, matrix, pieces=2):
    size = count // pieces
    results = []
    for at in range(pieces):
        rows = slice(row + at * size, row + (at + 1) * size)
        high, low = high_ref[rows, :], low_ref[rows, :]
        results.append(dot(jnp.concatenate([high, low, high], axis=1), matrix))
    return results


def last_stage(fine, back, twist):
    cos, sin = twist[:, :SIDE], twist[:, SIDE:]
    split = []
    for at in range(0, len(fine), 2):
        reals, imags = [], []
        for slab in fine[at : at + 2]:
            real, imag = slab[:, :SIDE], slab[:, SIDE:]
            reals.append(real * cos - imag * sin)
            imags.append(imag * cos + real * sin)
        turned = jnp.concatenate(
            [jnp.concatenate(reals, axis=1), jnp.concatenate(imags, axis=1)], axis=0
        )
        split.append(halves(turned))
    both = [dot(back, high) for high, _ in split]
    rest = [dot(back[:SIDE], low) for _, low in split]
    return [b[:SIDE] + b[SIDE:] + r for b, r in zip(both, rest)]


def slabs_of(parts):
    return [part[at : at + SIDE] for part in parts for at in range(0, part.shape[0], SIDE)]


def product(left, right):
    lr, li = left[:, :SIDE], left[:, SIDE:]
    rr, ri = right[:, :SIDE], right[:, SIDE:]
    return jnp.concatenate([lr * rr - li * ri, lr * ri + li * rr], axis=1)


def turned_product(left, right):
    lr, li = left[:, :SIDE], left[:, SIDE:]
    rr, ri = right[:, :SIDE], right[:, SIDE:]
    return jnp.concatenate([lr * rr + li * ri, lr * ri - li * rr], axis=1)


def gather_rows(ref, base, step, shards, pitch):
    return jnp.concatenate(
        [ref[pl.ds(base + q * step, shards, stride=pitch), :] for q in range(QUARTERS)], axis=0
    )


def pack_kernel(
    members, near_ref, k_hbm, v_hbm, g_hbm, q_hbm, f_hbm, out_ref,
    k_ref, v_ref, g_ref, q_ref, f_ref, sems,
):
    copies = []
    plan = ((k_hbm, k_ref, 0, 4), (v_hbm, v_ref, 0, 4))
    plan += ((g_hbm, g_ref, 0, 2), (q_hbm, q_ref, 0, 2), (g_hbm, g_ref, 2, 2), (q_hbm, q_ref, 2, 2))
    for at, (source, target, first, count) in enumerate(plan):
        rows = pl.ds(first * SIDE, count * SIDE)
        copy = pltpu.make_async_copy(source.at[rows], target.at[rows], sems.at[at])
        copy.start()
        copies.append(copy)
        if at == 1:
            start = pl.multiple_of(near_ref[0] * SIDE, SIDE)
            own = pltpu.make_async_copy(f_hbm.at[pl.ds(start, SIDE)], f_ref, sems.at[6])
            own.start()

    def put(array, left, right, quarters):
        for q in quarters:
            rows = slice(q * SIDE, (q + 1) * SIDE)
            for h in range(HALVES):
                cols = slice(h * SIDE, (h + 1) * SIDE)
                at = array * 8 + h * QUARTERS + q
                out_ref[pl.ds(at, members, stride=IN_ROWS), :] = (
                    left[rows, cols] * right[rows, cols]
                ).T

    copies[0].wait()
    copies[1].wait()
    put(0, k_ref, v_ref, range(QUARTERS))
    own.wait()
    out_ref[pl.ds(16, members, stride=IN_ROWS), :] = f_ref[...].T
    for part in range(2):
        copies[2 + part * 2].wait()
        copies[3 + part * 2].wait()
        put(1, g_ref, q_ref, (2 * part, 2 * part + 1))


def ahead_kernel(
    shards, in_ref, into_ref, back_ref, ahead_ref, behind_ref, twist_ref,
    corr_ref, gated_ref, grad_ref, high_ref, low_ref,
):
    into, twist = into_ref[...], twist_ref[...]
    pitch = shards * IN_ROWS
    span = BLOCKS * HALVES * SIDE
    half = span // 2
    total = None
    for part in range(2):
        for array in range(2):
            slabs = [
                gather_rows(
                    in_ref, block * pitch + array * 8 + h * QUARTERS, 1, shards, IN_ROWS
                )
                for block in (part * 2, part * 2 + 1)
                for h in range(HALVES)
            ]
            coarse_stage(slabs, into, twist, high_ref, low_ref, part * span + array * half)
    for part in range(2):
        both = fine_stage(high_ref, low_ref, part * span, span, ahead_ref[...], 1)[0]
        both = (both[:half], both[half:])
        rows = slice(part * half, (part + 1) * half)
        gated_ref[rows, :] = both[0]
        grad_ref[rows, :] = both[1]
        for at in range(0, half, SIDE):
            term = turned_product(both[0][at : at + SIDE], both[1][at : at + SIDE])
            total = term if total is None else total + term
    store_halves(total, high_ref, low_ref, 2 * span)
    fine = fine_stage(high_ref, low_ref, 2 * span, SIDE, behind_ref[...], 1)
    corr_ref[...] = last_stage([jnp.concatenate(fine, axis=0)], back_ref[...], twist)[0]


def behind_kernel(
    shards, in_ref, gated_ref, grad_ref, into_ref, back_ref, ahead_ref, behind_ref, twist_ref,
    out_ref, high_ref, low_ref,
):
    twist, back = twist_ref[...], back_ref[...]
    pitch = shards * OUT_ROWS
    group = 2 * HALVES * SIDE
    spare = BLOCKS * group
    slab = gather_rows(in_ref, 16, shards * IN_ROWS, shards, IN_ROWS)
    coarse_stage([slab], into_ref[...], twist, high_ref, low_ref, spare)
    filt = jnp.concatenate(fine_stage(high_ref, low_ref, spare, SIDE, ahead_ref[...]), axis=0)
    for block in range(BLOCKS):
        for array, spec_ref in enumerate((gated_ref, grad_ref)):
            combine = turned_product if array else product
            for h in range(HALVES):
                spec = spec_ref[pl.ds((block * 2 + h) * SIDE, SIDE), :]
                row = block * group + (array * HALVES + h) * SIDE
                store_halves(combine(filt, spec), high_ref, low_ref, row)
    for part in range(2):
        fine = slabs_of(
            fine_stage(high_ref, low_ref, part * 2 * group, 2 * group, behind_ref[...])
        )
        for near in range(2):
            block = part * 2 + near
            results = last_stage(fine[near * 4 : near * 4 + 4], back, twist)
            for at in range(2 * HALVES):
                column = at % 2 * SIDE
                for q in range(QUARTERS):
                    row = block * pitch + at * QUARTERS + q
                    out_ref[pl.ds(row, shards, stride=OUT_ROWS), :] = results[at // 2][
                        q * shards : (q + 1) * shards, column : column + SIDE
                    ]


def sum_kernel(shards, own_ref, other_ref, _, out_ref):
    total = own_ref[...] + other_ref[...]
    for block in range(BLOCKS):
        for q in range(QUARTERS):
            at = block * shards * OUT_ROWS + 16 + q
            out_ref[pl.ds(at, shards, stride=OUT_ROWS), :] = total[
                q * shards : (q + 1) * shards
            ]


def unpack_kernel(
    members, in_ref, g_ref, v_ref, k_ref, gq_hbm, gk_hbm, gv_hbm, gf_hbm,
    gq_ref, gk_ref, gv_ref, gf_ref, sems,
):
    copies = []

    def send(source, target, q):
        part = pl.ds(q * SIDE, SIDE)
        copy = pltpu.make_async_copy(source.at[part], target.at[part], sems.at[len(copies)])
        copy.start()
        copies.append(copy)

    for q in range(QUARTERS):
        rows = slice(q * SIDE, (q + 1) * SIDE)
        for h in range(HALVES):
            cols = slice(h * SIDE, (h + 1) * SIDE)
            back = in_ref[pl.ds(8 + h * QUARTERS + q, members, stride=OUT_ROWS), :].T
            gk_ref[rows, cols] = back * v_ref[rows, cols]
            gv_ref[rows, cols] = back * k_ref[rows, cols]
        send(gk_ref, gk_hbm, q)
        send(gv_ref, gv_hbm, q)
        for h in range(HALVES):
            cols = slice(h * SIDE, (h + 1) * SIDE)
            conv = in_ref[pl.ds(h * QUARTERS + q, members, stride=OUT_ROWS), :].T
            gq_ref[rows, cols] = conv * g_ref[rows, cols]
        send(gq_ref, gq_hbm, q)
        gf_ref[rows, :] = in_ref[pl.ds(16 + q, members, stride=OUT_ROWS), :].T
        send(gf_ref, gf_hbm, q)
    for copy in copies:
        copy.wait()


VMEM = pl.BlockSpec(memory_space=pltpu.VMEM)
HBM = pl.BlockSpec(memory_space=pltpu.HBM)
SMEM = pl.BlockSpec(memory_space=pltpu.SMEM)
LIMIT = 24 * 1024 * 1024


def call(kernel, outs, args, name, ins=None, out_spec=VMEM, scratch=(), flops=0, aliases=None):
    moved = sum(4 * int(np.prod(shape)) for shape in outs)
    moved += sum(a.size * a.dtype.itemsize for a in args)
    return pl.pallas_call(
        kernel,
        out_shape=[jax.ShapeDtypeStruct(shape, F32) for shape in outs],
        in_specs=ins or [VMEM] * len(args),
        out_specs=[out_spec] * len(outs),
        scratch_shapes=list(scratch),
        input_output_aliases=aliases or {},
        name=name,
        compiler_params=pltpu.CompilerParams(vmem_limit_bytes=LIMIT),
        cost_estimate=pl.CostEstimate(flops=flops, bytes_accessed=moved, transcendentals=0),
    )(*args)


def exchange(block, inner):
    parted = block.reshape(block.shape[0] // int(np.prod(inner)), *inner, SIDE)
    return lax.all_to_all(parted, ("near", "seq"), 0, 0, tiled=True).reshape(block.shape)


def local(q_gate, k_gate, values, filter_raw, grad_out):
    shards = lax.axis_size("seq")
    members = shards * lax.axis_size("near")
    total = SIDE * SIDE
    into, back, ahead, behind, twist = (
        jnp.asarray(t) for t in tables(shards, total ** (-0.5) / total)
    )
    block = q_gate.shape
    wide = pltpu.VMEM(block, F32)
    split = [pltpu.VMEM((17 * SIDE, 2 * SIDE), BF)] * 2
    near = lax.axis_index("near").astype(jnp.int32).reshape(1)
    packed = call(
        functools.partial(pack_kernel, members),
        [(IN_ROWS * members, SIDE)],
        (near, *(pltpu.with_memory_space_constraint(a, pltpu.HBM) for a in (k_gate, values, grad_out, q_gate, filter_raw))),
        "pack",
        ins=[SMEM] + [HBM] * 5,
        scratch=[wide] * 4 + [pltpu.VMEM((SIDE, SIDE), F32), pltpu.SemaphoreType.DMA((7,))],
    )[0]
    spread = exchange(packed, (17, 1))
    corr, gated_spec, grad_spec = call(
        functools.partial(ahead_kernel, shards),
        [(SIDE, SIDE), (8 * SIDE, 2 * SIDE), (8 * SIDE, 2 * SIDE)],
        (spread, into, back, ahead, behind, twist),
        "ahead",
        scratch=split,
        flops=10**9,
    )
    other = lax.ppermute(corr, "far", [(0, 1), (1, 0)])
    results = call(
        functools.partial(behind_kernel, shards),
        [(OUT_ROWS * members, SIDE)],
        (spread, gated_spec, grad_spec, into, back, ahead, behind, twist),
        "behind",
        scratch=split,
        flops=10**9,
    )[0]
    results = call(
        functools.partial(sum_kernel, shards),
        [(OUT_ROWS * members, SIDE)],
        (corr, other, results),
        "sum",
        ins=[VMEM] * 3,
        aliases={2: 0},
    )[0]
    placed = exchange(results, (5, 4))
    grad_q, grad_k, grad_v, grad_filter = call(
        functools.partial(unpack_kernel, members),
        [block, block, block, filter_raw.shape],
        (placed, grad_out, values, k_gate),
        "unpack",
        out_spec=HBM,
        scratch=[wide] * 3 + [pltpu.VMEM(filter_raw.shape, F32), pltpu.SemaphoreType.DMA((16,))],
    )
    return grad_q, grad_k, grad_v, grad_filter


def solution(mesh):
    shards, groups = mesh.devices.shape
    parted = Mesh(
        mesh.devices.reshape(shards, groups // BLOCKS, BLOCKS), ("seq", "far", "near")
    )
    whole, filters = P("seq", ("far", "near")), P("seq", None)
    return jax.shard_map(
        local,
        mesh=parted,
        in_specs=(whole, whole, whole, filters, whole),
        out_specs=(whole, whole, whole, filters),
        check_vma=False,
    )
```

```python
import functools

import jax
import jax.numpy as jnp
import numpy as np
from jax import lax
from jax.experimental import pallas as pl
from jax.experimental.pallas import tpu as pltpu
from jax.sharding import Mesh
from jax.sharding import PartitionSpec as P


SIDE = 128
HALVES = 2
BLOCKS = 4
QUARTERS = 4
IN_ROWS = 17
OUT_ROWS = 20
BF = jnp.bfloat16
F32 = jnp.float32


def split_np(table):
    high = table.astype(np.float32).astype(BF)
    low = (table - high.astype(np.float64)).astype(np.float32).astype(BF)
    return high, low


def tables(shards, factor):
    total = SIDE * SIDE
    index = np.arange(SIDE)
    quarter, source = np.divmod(index, shards)
    first = source * QUARTERS + quarter
    coarse = 2.0 * np.pi * np.outer(index + 0.25, first) / SIDE
    high, low = split_np(np.concatenate([np.cos(coarse), -np.sin(coarse)], axis=0))
    into = np.concatenate([high, low, high], axis=1)
    high, low = split_np(np.concatenate([np.cos(coarse.T), -np.sin(coarse.T)], axis=1) * factor)
    back = np.concatenate([high, low], axis=0)
    fine = 2.0 * np.pi * (np.outer(index, index) % SIDE) / SIDE
    cos, sin = np.cos(fine), np.sin(fine)
    high, low = split_np(np.block([[cos, -sin], [sin, cos]]))
    ahead = np.concatenate([high, high, low], axis=0)
    high, low = split_np(np.block([[cos, sin], [-sin, cos]]))
    behind = np.concatenate([high, high, low], axis=0)
    turn = 2.0 * np.pi * np.outer(index + 0.25, index) / total
    twist = np.concatenate([np.cos(turn), np.sin(turn)], axis=1).astype(np.float32)
    return into, back, ahead, behind, twist


def halves(value):
    high = value.astype(BF)
    return high, (value - high.astype(F32)).astype(BF)


def dot(left, right):
    return jnp.dot(left, right, preferred_element_type=F32)


def coarse_stage(slabs, into, twist, high_ref, low_ref, row):
    high, low = halves(jnp.concatenate(slabs, axis=1))
    coarse = dot(into, jnp.concatenate([high, high, low], axis=0))
    cos, sin = twist[:, :SIDE], twist[:, SIDE:]
    for at in range(len(slabs)):
        real = coarse[:SIDE, at * SIDE : (at + 1) * SIDE]
        imag = coarse[SIDE:, at * SIDE : (at + 1) * SIDE]
        store_halves(
            jnp.concatenate([real * cos + imag * sin, imag * cos - real * sin], axis=1),
            high_ref, low_ref, row + at * SIDE,
        )


def store_halves(value, high_ref, low_ref, row):
    high, low = halves(value)
    rows = slice(row, row + value.shape[0])
    high_ref[rows, :] = high
    low_ref[rows, :] = low


def fine_stage(high_ref, low_ref, row, count, matrix, pieces=2):
    size = count // pieces
    results = []
    for at in range(pieces):
        rows = slice(row + at * size, row + (at + 1) * size)
        high, low = high_ref[rows, :], low_ref[rows, :]
        results.append(dot(jnp.concatenate([high, low, high], axis=1), matrix))
    return results


def last_stage(fine, back, twist):
    cos, sin = twist[:, :SIDE], twist[:, SIDE:]
    split = []
    for at in range(0, len(fine), 2):
        reals, imags = [], []
        for slab in fine[at : at + 2]:
            real, imag = slab[:, :SIDE], slab[:, SIDE:]
            reals.append(real * cos - imag * sin)
            imags.append(imag * cos + real * sin)
        turned = jnp.concatenate(
            [jnp.concatenate(reals, axis=1), jnp.concatenate(imags, axis=1)], axis=0
        )
        split.append(halves(turned))
    both = [dot(back, high) for high, _ in split]
    rest = [dot(back[:SIDE], low) for _, low in split]
    return [b[:SIDE] + b[SIDE:] + r for b, r in zip(both, rest)]


def slabs_of(parts):
    return [part[at : at + SIDE] for part in parts for at in range(0, part.shape[0], SIDE)]


def product(left, right):
    lr, li = left[:, :SIDE], left[:, SIDE:]
    rr, ri = right[:, :SIDE], right[:, SIDE:]
    return jnp.concatenate([lr * rr - li * ri, lr * ri + li * rr], axis=1)


def turned_product(left, right):
    lr, li = left[:, :SIDE], left[:, SIDE:]
    rr, ri = right[:, :SIDE], right[:, SIDE:]
    return jnp.concatenate([lr * rr + li * ri, lr * ri - li * rr], axis=1)


def gather_rows(ref, base, step, shards, pitch):
    return jnp.concatenate(
        [ref[pl.ds(base + q * step, shards, stride=pitch), :] for q in range(QUARTERS)], axis=0
    )


def pack_kernel(
    members, near_ref, k_hbm, v_hbm, g_hbm, q_hbm, f_hbm, out_ref,
    k_ref, v_ref, g_ref, q_ref, f_ref, sems,
):
    copies = []
    for part in range(2):
        rows = pl.ds(part * 2 * SIDE, 2 * SIDE)
        pairs = ((k_hbm, k_ref), (v_hbm, v_ref), (g_hbm, g_ref), (q_hbm, q_ref))
        for at, (source, target) in enumerate(pairs):
            copy = pltpu.make_async_copy(source.at[rows], target.at[rows], sems.at[part * 4 + at])
            copy.start()
            copies.append(copy)
        if part == 0:
            start = pl.multiple_of(near_ref[0] * SIDE, SIDE)
            own = pltpu.make_async_copy(f_hbm.at[pl.ds(start, SIDE)], f_ref, sems.at[16])
            own.start()
    for part in range(2):
        for array, (left, right) in enumerate(((k_ref, v_ref), (g_ref, q_ref))):
            copies[part * 4 + array * 2].wait()
            copies[part * 4 + array * 2 + 1].wait()
            for q in (2 * part, 2 * part + 1):
                rows = slice(q * SIDE, (q + 1) * SIDE)
                for h in range(HALVES):
                    cols = slice(h * SIDE, (h + 1) * SIDE)
                    at = array * 8 + h * QUARTERS + q
                    out_ref[pl.ds(at, members, stride=IN_ROWS), :] = (
                        left[rows, cols] * right[rows, cols]
                    ).T
        if part == 0:
            own.wait()
            out_ref[pl.ds(16, members, stride=IN_ROWS), :] = f_ref[...].T


def ahead_kernel(
    shards, in_ref, into_ref, back_ref, ahead_ref, behind_ref, twist_ref,
    corr_ref, gated_ref, grad_ref, high_ref, low_ref,
):
    into, twist = into_ref[...], twist_ref[...]
    pitch = shards * IN_ROWS
    span = BLOCKS * HALVES * SIDE
    half = span // 2
    total = None
    for part in range(2):
        for array in range(2):
            slabs = [
                gather_rows(
                    in_ref, block * pitch + array * 8 + h * QUARTERS, 1, shards, IN_ROWS
                )
                for block in (part * 2, part * 2 + 1)
                for h in range(HALVES)
            ]
            coarse_stage(slabs, into, twist, high_ref, low_ref, part * span + array * half)
    for part in range(2):
        both = fine_stage(high_ref, low_ref, part * span, span, ahead_ref[...], 1)[0]
        both = (both[:half], both[half:])
        rows = slice(part * half, (part + 1) * half)
        gated_ref[rows, :] = both[0]
        grad_ref[rows, :] = both[1]
        for at in range(0, half, SIDE):
            term = turned_product(both[0][at : at + SIDE], both[1][at : at + SIDE])
            total = term if total is None else total + term
    store_halves(total, high_ref, low_ref, 2 * span)
    fine = fine_stage(high_ref, low_ref, 2 * span, SIDE, behind_ref[...], 1)
    corr_ref[...] = last_stage([jnp.concatenate(fine, axis=0)], back_ref[...], twist)[0]


def behind_kernel(
    shards, in_ref, gated_ref, grad_ref, into_ref, back_ref, ahead_ref, behind_ref, twist_ref,
    out_ref, high_ref, low_ref,
):
    twist, back = twist_ref[...], back_ref[...]
    pitch = shards * OUT_ROWS
    group = 2 * HALVES * SIDE
    spare = BLOCKS * group
    slab = gather_rows(in_ref, 16, shards * IN_ROWS, shards, IN_ROWS)
    coarse_stage([slab], into_ref[...], twist, high_ref, low_ref, spare)
    filt = jnp.concatenate(fine_stage(high_ref, low_ref, spare, SIDE, ahead_ref[...]), axis=0)
    for block in range(BLOCKS):
        for array, spec_ref in enumerate((gated_ref, grad_ref)):
            combine = turned_product if array else product
            for h in range(HALVES):
                spec = spec_ref[pl.ds((block * 2 + h) * SIDE, SIDE), :]
                row = block * group + (array * HALVES + h) * SIDE
                store_halves(combine(filt, spec), high_ref, low_ref, row)
    for part in range(2):
        fine = slabs_of(
            fine_stage(high_ref, low_ref, part * 2 * group, 2 * group, behind_ref[...])
        )
        for near in range(2):
            block = part * 2 + near
            results = last_stage(fine[near * 4 : near * 4 + 4], back, twist)
            for at in range(2 * HALVES):
                column = at % 2 * SIDE
                for q in range(QUARTERS):
                    row = block * pitch + at * QUARTERS + q
                    out_ref[pl.ds(row, shards, stride=OUT_ROWS), :] = results[at // 2][
                        q * shards : (q + 1) * shards, column : column + SIDE
                    ]


def sum_kernel(shards, own_ref, other_ref, _, out_ref):
    total = own_ref[...] + other_ref[...]
    for block in range(BLOCKS):
        for q in range(QUARTERS):
            at = block * shards * OUT_ROWS + 16 + q
            out_ref[pl.ds(at, shards, stride=OUT_ROWS), :] = total[
                q * shards : (q + 1) * shards
            ]


def unpack_kernel(
    members, in_ref, g_ref, v_ref, k_ref, gq_hbm, gk_hbm, gv_hbm, gf_hbm,
    gq_ref, gk_ref, gv_ref, gf_ref, sems,
):
    copies = []

    def send(source, target, q):
        part = pl.ds(q * SIDE, SIDE)
        copy = pltpu.make_async_copy(source.at[part], target.at[part], sems.at[len(copies)])
        copy.start()
        copies.append(copy)

    for q in range(QUARTERS):
        rows = slice(q * SIDE, (q + 1) * SIDE)
        gf_ref[rows, :] = in_ref[pl.ds(16 + q, members, stride=OUT_ROWS), :].T
        send(gf_ref, gf_hbm, q)
        for h in range(HALVES):
            cols = slice(h * SIDE, (h + 1) * SIDE)
            back = in_ref[pl.ds(8 + h * QUARTERS + q, members, stride=OUT_ROWS), :].T
            gk_ref[rows, cols] = back * v_ref[rows, cols]
            gv_ref[rows, cols] = back * k_ref[rows, cols]
        send(gk_ref, gk_hbm, q)
        send(gv_ref, gv_hbm, q)
        for h in range(HALVES):
            cols = slice(h * SIDE, (h + 1) * SIDE)
            conv = in_ref[pl.ds(h * QUARTERS + q, members, stride=OUT_ROWS), :].T
            gq_ref[rows, cols] = conv * g_ref[rows, cols]
        send(gq_ref, gq_hbm, q)
    for copy in copies:
        copy.wait()


VMEM = pl.BlockSpec(memory_space=pltpu.VMEM)
HBM = pl.BlockSpec(memory_space=pltpu.HBM)
SMEM = pl.BlockSpec(memory_space=pltpu.SMEM)
LIMIT = 24 * 1024 * 1024


def call(kernel, outs, args, name, ins=None, out_spec=VMEM, scratch=(), flops=0, aliases=None):
    moved = sum(4 * int(np.prod(shape)) for shape in outs)
    moved += sum(a.size * a.dtype.itemsize for a in args)
    return pl.pallas_call(
        kernel,
        out_shape=[jax.ShapeDtypeStruct(shape, F32) for shape in outs],
        in_specs=ins or [VMEM] * len(args),
        out_specs=[out_spec] * len(outs),
        scratch_shapes=list(scratch),
        input_output_aliases=aliases or {},
        name=name,
        compiler_params=pltpu.CompilerParams(vmem_limit_bytes=LIMIT),
        cost_estimate=pl.CostEstimate(flops=flops, bytes_accessed=moved, transcendentals=0),
    )(*args)


def exchange(block, inner):
    parted = block.reshape(block.shape[0] // int(np.prod(inner)), *inner, SIDE)
    return lax.all_to_all(parted, ("near", "seq"), 0, 0, tiled=True).reshape(block.shape)


def local(q_gate, k_gate, values, filter_raw, grad_out):
    shards = lax.axis_size("seq")
    members = shards * lax.axis_size("near")
    total = SIDE * SIDE
    into, back, ahead, behind, twist = (
        jnp.asarray(t) for t in tables(shards, total ** (-0.5) / total)
    )
    block = q_gate.shape
    wide = pltpu.VMEM(block, F32)
    split = [pltpu.VMEM((17 * SIDE, 2 * SIDE), BF)] * 2
    near = lax.axis_index("near").astype(jnp.int32).reshape(1)
    packed = call(
        functools.partial(pack_kernel, members),
        [(IN_ROWS * members, SIDE)],
        (near, *(pltpu.with_memory_space_constraint(a, pltpu.HBM) for a in (k_gate, values, grad_out, q_gate, filter_raw))),
        "pack",
        ins=[SMEM] + [HBM] * 5,
        scratch=[wide] * 4 + [pltpu.VMEM((SIDE, SIDE), F32), pltpu.SemaphoreType.DMA((17,))],
    )[0]
    spread = exchange(packed, (17, 1))
    corr, gated_spec, grad_spec = call(
        functools.partial(ahead_kernel, shards),
        [(SIDE, SIDE), (8 * SIDE, 2 * SIDE), (8 * SIDE, 2 * SIDE)],
        (spread, into, back, ahead, behind, twist),
        "ahead",
        scratch=split,
        flops=10**9,
    )
    other = lax.ppermute(corr, "far", [(0, 1), (1, 0)])
    results = call(
        functools.partial(behind_kernel, shards),
        [(OUT_ROWS * members, SIDE)],
        (spread, gated_spec, grad_spec, into, back, ahead, behind, twist),
        "behind",
        scratch=split,
        flops=10**9,
    )[0]
    results = call(
        functools.partial(sum_kernel, shards),
        [(OUT_ROWS * members, SIDE)],
        (corr, other, results),
        "sum",
        ins=[VMEM] * 3,
        aliases={2: 0},
    )[0]
    placed = exchange(results, (5, 4))
    grad_q, grad_k, grad_v, grad_filter = call(
        functools.partial(unpack_kernel, members),
        [block, block, block, filter_raw.shape],
        (placed, grad_out, values, k_gate),
        "unpack",
        out_spec=HBM,
        scratch=[wide] * 3 + [pltpu.VMEM(filter_raw.shape, F32), pltpu.SemaphoreType.DMA((16,))],
    )
    return grad_q, grad_k, grad_v, grad_filter


def solution(mesh):
    shards, groups = mesh.devices.shape
    parted = Mesh(
        mesh.devices.reshape(shards, groups // BLOCKS, BLOCKS), ("seq", "far", "near")
    )
    whole, filters = P("seq", ("far", "near")), P("seq", None)
    return jax.shard_map(
        local,
        mesh=parted,
        in_specs=(whole, whole, whole, filters, whole),
        out_specs=(whole, whole, whole, filters),
        check_vma=False,
    )
```
